512 devices in a mesh: section: 16 (over z, core), tp: 32 (over x, y).
Axes of the slice: x: 4, y: 8, z: 8, core: 2. Of those that a mesh axis runs over, the one named last changes fastest.
Arguments:
- hidden: bfloat16 [16, 256, 8192], P('section', 'tp'), may hold values from -6 to 6
- norm_gain: float32 [16, 8192], P('section'), may hold values from 0.1 to 1.9
- w_query: bfloat16 [16, 8192, 4096], P('section', None, 'tp'), may hold values from -0.0625 to 0.0625
- w_keyval: bfloat16 [16, 1024, 8192], P('section', 'tp'), may hold values from -0.0625 to 0.0625
- w_out: bfloat16 [16, 4096, 8192], P('section', 'tp'), may hold values from -0.09375 to 0.09375
- kv_cache: bfloat16 [16, 128, 24, 1024], P('section', 'tp'), may hold values from -700 to 700
- owner_map: int32 [16, 64], P('section'), may hold values from 0 to 31, as said below
- accepted: int32 [16, 64], P('section'), may hold values from 0 to 4
- context: int32 [16, 64], P('section'), may hold values from 1 to 24
- draft_ids: int32 [16, 64, 4], P('section'), may hold values from 0 to 151935
Outputs:
- next_hidden: bfloat16 [16, 256, 8192], P('section', 'tp')
- committed_kv: bfloat16 [16, 512, 1024], P('section', 'tp')
- committed_ids: int32 [16, 512], P('section', 'tp')
The draws below stay inside these ranges and needn't reach their ends.
Inputs may be any that keep to these rules, and one draw needn't show every extreme that they name: `owner_map`: in every window at most 4 requests share an owner, and some owner holds exactly 4.
All inputs are finite; a program needn't handle non-finite values.
Results may differ from the reference program's by a relative error of at most 0.017.
Values may be sent and summed in bfloat16 or wider, within the bound.
A program may use at most 64 MiB of HBM per device.

```python
import jax
import jax.numpy as jnp
from jax import lax

D = 8192
HEADS = 32
KVH = 4
HD = 128
K_DRAFT = 4
REQ_DEV = 2
CTX = 24
KVW = 512
SECTIONS = 16
GROUPS = 32
CAPR = 4
REQ = 64
TOKENS = 256


def owners_for_section(section_key):
    groups = REQ // REQ_DEV
    slot_total = groups * CAPR
    key_full, key_order, key_assign = jax.random.split(section_key, 3)
    busiest = jax.random.randint(key_full, (), 0, groups)
    ranking = jax.random.permutation(key_order, slot_total).astype(jnp.int32)
    slot_owner = jnp.arange(slot_total, dtype=jnp.int32) // CAPR
    ranking = jnp.where(slot_owner == busiest, ranking - slot_total, ranking)
    ordered = jnp.argsort(ranking, stable=True)
    chosen = jax.random.permutation(key_assign, ordered[:REQ])
    return (chosen // CAPR).astype(jnp.int32)


def draw_owner_map(key, part):
    section_keys = jax.random.split(jax.random.fold_in(key, 11), SECTIONS)
    return jax.vmap(owners_for_section)(section_keys)


def draw_context(key, part):
    key_base, key_pick = jax.random.split(jax.random.fold_in(key, 23))
    lengths = jax.random.randint(key_base, (SECTIONS, REQ), 1, CTX + 1)
    chosen = jax.random.randint(key_pick, (SECTIONS, 1), 0, REQ)
    column = jnp.arange(REQ)[None, :]
    return jnp.where(column == chosen, CTX, lengths).astype(jnp.int32)


def draw_kv_cache(key, part):
    full_shape = (SECTIONS, GROUPS * CAPR, CTX, 2 * KVW)
    key_base = jax.random.fold_in(jax.random.fold_in(key, 37), 0)
    return jax.random.normal(key_base, full_shape, jnp.float32).astype(jnp.bfloat16)


def touch_ends(array, own_key, smallest, top_value):
    longest = array.shape.index(max(array.shape))
    spots = []
    for shift in (0, 1):
        where = [jax.random.randint(jax.random.fold_in(own_key, axis), (), 0, length) for axis, length in enumerate(array.shape)]
        where[longest] = (where[longest] + shift) % array.shape[longest]
        spots.append(tuple(where))
    return array.at[spots[0]].set(smallest).at[spots[1]].set(top_value)


def levels(stream_key, dims, cuts, least, largest):
    loudness = 1.0
    for dim, shards_of in cuts:
        steps = jax.random.uniform(jax.random.fold_in(jax.random.fold_in(stream_key, 6), dim), (shards_of,), jnp.float32, least / len(cuts), largest / len(cuts))
        loudness = loudness * jnp.repeat(jnp.exp(steps), dims[dim] // shards_of).reshape((-1,) + (1,) * (len(dims) - 1 - dim))
    return loudness


def noise(stream_key, extent, spread, most, pieces=(), kind=jnp.bfloat16):
    level = levels(stream_key, extent, pieces, -0.22, 0.18) if pieces else 1.0
    values = jax.random.normal(stream_key, extent, jnp.float32) * spread * level
    return jnp.minimum(jnp.maximum(values, -most), most).astype(kind)


def setup_inputs(seed: int = 0) -> dict:
    splits = jax.random.split(jax.random.key(seed), 11)
    hidden = noise(splits[0], (SECTIONS, TOKENS, D), 1.0, 6.0, ((0, 16), (1, 32)))
    norm_gain = jnp.clip(1.0 + 0.18 * jax.random.normal(splits[1], (SECTIONS, D), jnp.float32), 0.1, 1.9)
    w_query = noise(splits[2], (SECTIONS, D, HEADS * HD), D ** -0.5, 0.0625, ((0, 16), (2, 32)))
    w_keyval = noise(splits[3], (SECTIONS, 2 * KVW, D), D ** -0.5, 0.0625, ((0, 16), (1, 32)))
    w_out = noise(splits[4], (SECTIONS, HEADS * HD, D), (HEADS * HD) ** -0.5, 0.09375, ((0, 16), (1, 32)))
    kv_cache = draw_kv_cache(jax.random.fold_in(splits[10], 71), 0)
    owner_map = draw_owner_map(jax.random.fold_in(splits[10], 71), 0)
    accepted = touch_ends(jax.random.randint(splits[7], (SECTIONS, REQ), 0, K_DRAFT + 1), jax.random.fold_in(splits[7], 1), 0, K_DRAFT).astype(jnp.int32)
    context = draw_context(jax.random.fold_in(splits[10], 71), 0)
    draft_ids = touch_ends(jax.random.randint(splits[9], (SECTIONS, REQ, K_DRAFT), 0, 151936), jax.random.fold_in(splits[9], 1), 0, 151935).astype(jnp.int32)
    return {"hidden": hidden, "norm_gain": norm_gain, "w_query": w_query, "w_keyval": w_keyval, "w_out": w_out, "kv_cache": kv_cache, "owner_map": owner_map, "accepted": accepted, "context": context, "draft_ids": draft_ids}


epsilon = 1e-06

def owner_ranks(owners):
    count_all = owners.shape[0]
    same_owner = owners[:, None] == owners[None, :]
    position = jnp.arange(count_all, dtype=jnp.int32)
    earlier = position[None, :] < position[:, None]
    return lax.optimization_barrier(jnp.sum(jnp.where(same_owner & earlier, 1, 0), axis=1)).astype(jnp.int32)

def slot_requests(owners, capacity, groups):
    slot_of = owners * capacity + owner_ranks(owners)
    slot_total = groups * capacity
    matches = slot_of[None, :] == jnp.arange(slot_total, dtype=jnp.int32)[:, None]
    request_ids = jnp.arange(owners.shape[0], dtype=jnp.int32)
    found_ids = lax.optimization_barrier(jnp.sum(jnp.where(matches, request_ids[None, :] + 1, 0), axis=1))
    return (found_ids - 1).astype(jnp.int32)

def attend(queries, new_pairs, cached, lengths):
    slot_count = queries.shape[0]
    draft_steps = queries.shape[1]
    cached_len = cached.shape[1]
    pair_width = cached.shape[2] // 2
    key_span = cached_len + draft_steps
    key_rows = jnp.concatenate([cached[:, :, :pair_width], new_pairs[:, :, :pair_width]], axis=1)
    values = jnp.concatenate([cached[:, :, pair_width:], new_pairs[:, :, pair_width:]], axis=1)
    key_rows = key_rows.reshape(slot_count, key_span, KVH, HD).astype(jnp.float32)
    values = values.reshape(slot_count, key_span, KVH, HD).astype(jnp.float32)
    grouped = queries.reshape(slot_count, draft_steps, KVH, HEADS // KVH, HD).astype(jnp.float32)
    scores = jnp.einsum('sjkgd,spkd->skgjp', grouped, key_rows) * HD ** (-0.5)
    position = jnp.arange(key_span, dtype=jnp.int32)
    step_ids = jnp.arange(draft_steps, dtype=jnp.int32)
    cached_ok = (position[None, :] < lengths[:, None]) & (position[None, :] < cached_len)
    fresh_ok = (position[None, :] >= cached_len) & (position[None, :] - cached_len <= step_ids[:, None])
    allowed = cached_ok[:, None, :] | fresh_ok[None, :, :]
    scores = jnp.where(allowed[:, None, None, :, :], scores, -jnp.inf)
    row_max = lax.optimization_barrier(jnp.max(scores, axis=-1, keepdims=True))
    weights = jnp.exp(scores - row_max)
    probabilities = (weights / lax.optimization_barrier(jnp.sum(weights, axis=-1, keepdims=True))).astype(jnp.bfloat16)
    attended = jnp.einsum('skgjp,spkd->sjkgd', probabilities.astype(jnp.float32), values)
    return attended.reshape(slot_count, draft_steps, HEADS * HD).astype(jnp.bfloat16)

def section_step(hidden, gain_row, w_query, w_keyval, w_out, kv_cache, owners, accepted, context, draft_ids):
    requests = owners.shape[0]
    draft_steps = draft_ids.shape[1]
    tokens = hidden.shape[0]
    capacity = kv_cache.shape[0] // GROUPS
    rows_f32 = hidden.astype(jnp.float32)
    inverse_rms = lax.rsqrt(lax.optimization_barrier(jnp.mean(rows_f32 * rows_f32, axis=1, keepdims=True)) + epsilon)
    normed = (rows_f32 * inverse_rms * gain_row[None, :]).astype(jnp.bfloat16)
    queries = jnp.dot(normed, w_query, preferred_element_type=jnp.float32).astype(jnp.bfloat16)
    new_pairs = lax.dot_general(normed, w_keyval, (((1,), (1,)), ((), ())), preferred_element_type=jnp.float32).astype(jnp.bfloat16)
    slot_of = owners * capacity + owner_ranks(owners)
    cached = jnp.take(kv_cache, slot_of, axis=0)
    attended = attend(queries.reshape(requests, draft_steps, HEADS * HD), new_pairs.reshape(requests, draft_steps, 2 * KVW), cached, context)
    heads_out = attended.reshape(tokens, HEADS * HD)
    group_cols = HEADS * HD // GROUPS

    def add_group(running, group_id):
        head_part = lax.dynamic_slice_in_dim(heads_out, group_id * group_cols, group_cols, 1)
        weight = lax.dynamic_slice_in_dim(w_out, group_id * group_cols, group_cols, 0)
        group_sum = jnp.dot(head_part, weight, preferred_element_type=jnp.float32).astype(jnp.bfloat16)
        return (running + lax.optimization_barrier(group_sum).astype(jnp.float32), None)
    summed, unused = lax.scan(add_group, jnp.zeros((tokens, D), jnp.float32), jnp.arange(GROUPS, dtype=jnp.int32))
    updated = (rows_f32 + summed).astype(jnp.bfloat16)
    holders = slot_requests(owners, capacity, GROUPS)
    live_slots = holders >= 0
    safe_req = jnp.maximum(holders, 0)
    pair_rows = jnp.take(new_pairs.reshape(requests, draft_steps, 2 * KVW), safe_req, axis=0)
    step_ids = jnp.arange(draft_steps, dtype=jnp.int32)
    keep_mask = live_slots[:, None] & (step_ids[None, :] < jnp.take(accepted, safe_req)[:, None])
    committed = jnp.where(keep_mask[:, :, None], pair_rows, jnp.zeros_like(pair_rows)).reshape(-1, 2 * KVW)
    kept_ids = jnp.where(keep_mask, jnp.take(draft_ids, safe_req, axis=0), -1).reshape(-1).astype(jnp.int32)
    return (updated, committed, kept_ids)

def reference(hidden, norm_gain, w_query, w_keyval, w_out, kv_cache, owner_map, accepted, context, draft_ids):
    updated, committed, kept_ids = lax.map(lambda section_parts: section_step(*section_parts), (hidden, norm_gain, w_query, w_keyval, w_out, kv_cache, owner_map, accepted, context, draft_ids))
    return (jnp.roll(updated, 1, axis=0), committed, kept_ids)
```

```python
import jax
import jax.numpy as jnp
from jax import lax
from jax.experimental import pallas as pl
from jax.experimental.pallas import tpu as pltpu
from jax.sharding import PartitionSpec as P

HEADS = 32
KVH = 4
HD = 128


epsilon = 1e-06


NX = 4
NY = 8
LANES = 128
XY_SHARE = 26 / 64


def splits(width):
    first = max(1, round(width // LANES * XY_SHARE)) * LANES
    return ((0, first), (first, width - first))


def far_positive(mode, axis, dx, dy):
    if mode == 0:
        return True if axis == 0 else dx % 2 == 0
    return dy % 2 == 0 if axis == 0 else False


def reach(mode, axis, sign, dx, dy):
    half = (NX if axis == 0 else NY) // 2
    return half if far_positive(mode, axis, dx, dy) == (sign > 0) else half - 1


def travelled(mode, axis, dx, dy):
    size = NX if axis == 0 else NY
    ahead = (-dx if axis == 0 else -dy) % size
    if ahead == 0:
        return 0
    if ahead <= reach(mode, axis, 1, dx, dy):
        return ahead
    return ahead - size


def children(mode, dx, dy):
    first, second = (0, 1) if mode == 0 else (1, 0)
    hops = []
    step1 = travelled(mode, first, dx, dy)
    step2 = travelled(mode, second, dx, dy)
    if step2 == 0:
        for sign in (1, -1):
            if step1 * sign >= 0 and abs(step1) < reach(mode, first, sign, dx, dy):
                hops.append((first, sign))
    for sign in (1, -1):
        if step2 * sign >= 0 and abs(step2) < reach(mode, second, sign, dx, dy):
            hops.append((second, sign))
    return hops


def moved(axis, sign, dx, dy):
    return ((dx - sign) % NX, dy) if axis == 0 else (dx, (dy - sign) % NY)


def parent(mode, dx, dy):
    first, second = (0, 1) if mode == 0 else (1, 0)
    step2 = travelled(mode, second, dx, dy)
    axis = second if step2 else first
    return (axis, 1 if travelled(mode, axis, dx, dy) > 0 else -1)


def arrival_order(weights):
    free = {}
    order = []
    pending = [(0.0, 0, 0, 0), (0.0, 1, 0, 0)]
    while pending:
        pending.sort()
        now, mode, dx, dy = pending.pop(0)
        order.append((mode, dx, dy))
        for axis, sign in children(mode, dx, dy):
            begin = max(now, free.get((axis, sign), 0.0))
            free[axis, sign] = begin + weights[mode]
            pending.append((begin + weights[mode] + 1.6, mode) + moved(axis, sign, dx, dy))
    return order


def place_of(dx, dy):
    return dx * NY + dy


def neighbours(mx, my):
    return {
        (0, 1): lax.rem(mx + 1, NX) * NY + my,
        (0, -1): lax.rem(mx + NX - 1, NX) * NY + my,
        (1, 1): mx * NY + lax.rem(my + 1, NY),
        (1, -1): mx * NY + lax.rem(my + NY - 1, NY),
    }


def greet(devices):
    barrier = pltpu.get_barrier_semaphore()
    for device in devices:
        pl.semaphore_signal(
            barrier, inc=1, device_id={"tp": device}, device_id_type=pl.DeviceIdType.MESH
        )
    pl.semaphore_wait(barrier, len(devices))


def block_at(mx, my, dx, dy):
    return lax.rem(mx + dx, NX) * NY + lax.rem(my + dy, NY)


def gather_kernel(x_ref, out_ref, send_sems, recv_sems):
    me = lax.axis_index("tp")
    mx = me // NY
    my = lax.rem(me, NY)
    near = neighbours(mx, my)
    parts = splits(x_ref.shape[1])
    greet(list(near.values()))

    def copy(mode, dx, dy, link):
        start, width = parts[mode]
        there = moved(*link, dx, dy)
        cols = pl.ds(start, width)
        block = block_at(mx, my, dx, dy)
        source = x_ref.at[:, cols] if (dx, dy) == (0, 0) else out_ref.at[block, :, cols]
        return pltpu.make_async_remote_copy(
            src_ref=source,
            dst_ref=out_ref.at[block, :, cols],
            send_sem=send_sems.at[mode, place_of(*there)],
            recv_sem=recv_sems.at[mode, place_of(*there)],
            device_id={"tp": near[link]},
            device_id_type=pl.DeviceIdType.MESH,
        )

    started = []
    order = arrival_order([part[1] * 16 / 46e3 for part in parts])
    for mode, dx, dy in order:
        if (dx, dy) != (0, 0):
            link = parent(mode, dx, dy)
            start, width = parts[mode]
            cols = pl.ds(start, width)
            block = block_at(mx, my, dx, dy)
            pltpu.make_async_remote_copy(
                src_ref=out_ref.at[block, :, cols],
                dst_ref=out_ref.at[block, :, cols],
                send_sem=send_sems.at[mode, place_of(dx, dy)],
                recv_sem=recv_sems.at[mode, place_of(dx, dy)],
                device_id={"tp": near[link]},
                device_id_type=pl.DeviceIdType.MESH,
            ).wait_recv()
        for link in children(mode, dx, dy):
            sent = copy(mode, dx, dy, link)
            sent.start()
            started.append(sent)
    out_ref[me] = x_ref[...]
    for sent in started:
        sent.wait_send()


def gather_rows(rows):
    count, width = rows.shape
    groups = NX * NY
    out = pl.pallas_call(
        gather_kernel,
        out_shape=jax.ShapeDtypeStruct((groups, count, width), rows.dtype),
        in_specs=[pl.BlockSpec(memory_space=pltpu.VMEM)],
        out_specs=pl.BlockSpec(memory_space=pltpu.VMEM),
        scratch_shapes=[
            pltpu.SemaphoreType.DMA((2, groups)),
            pltpu.SemaphoreType.DMA((2, groups)),
        ],
        compiler_params=pltpu.CompilerParams(collective_id=0, has_side_effects=True),
    )(rows)
    return out.reshape(groups * count, width)


def reduce_kernel(p_ref, hid_ref, out_ref, got0, got1, stage0, stage1, send_sems, recv_sems):
    me = lax.axis_index("tp")
    mx = me // NY
    my = lax.rem(me, NY)
    near = neighbours(mx, my)
    parts = splits(hid_ref.shape[1])
    got = (got0, got1)
    stage = (stage0, stage1)
    greet(list(near.values()))
    started = []

    def total(mode, dx, dy):
        start, width = parts[mode]
        block = block_at(mx, my, dx, dy)
        summed = p_ref[block, :, pl.ds(start, width)].astype(jnp.float32)
        for link in children(mode, dx, dy):
            slot = place_of(*moved(*link, dx, dy))
            pltpu.make_async_remote_copy(
                src_ref=stage[mode].at[slot],
                dst_ref=got[mode].at[slot],
                send_sem=send_sems.at[mode, slot],
                recv_sem=recv_sems.at[mode, slot],
                device_id={"tp": near[link]},
                device_id_type=pl.DeviceIdType.MESH,
            ).wait_recv()
            summed = summed + got[mode][slot].astype(jnp.float32)
        return summed

    order = arrival_order([part[1] * 16 / 46e3 for part in parts])
    for mode, dx, dy in reversed(order):
        start, width = parts[mode]
        if (dx, dy) == (0, 0):
            cols = pl.ds(start, width)
            summed = total(mode, dx, dy) + hid_ref[:, cols].astype(jnp.float32)
            out_ref[:, cols] = summed.astype(out_ref.dtype)
            continue
        slot = place_of(dx, dy)
        if children(mode, dx, dy):
            stage[mode][slot] = total(mode, dx, dy).astype(jnp.bfloat16)
            source = stage[mode].at[slot]
        else:
            source = p_ref.at[block_at(mx, my, dx, dy), :, pl.ds(start, width)]
        axis, sign = parent(mode, dx, dy)
        sent = pltpu.make_async_remote_copy(
            src_ref=source,
            dst_ref=got[mode].at[slot],
            send_sem=send_sems.at[mode, slot],
            recv_sem=recv_sems.at[mode, slot],
            device_id={"tp": near[axis, -sign]},
            device_id_type=pl.DeviceIdType.MESH,
        )
        sent.start()
        started.append(sent)
    for sent in started:
        sent.wait_send()


def reduce_rows(product, residual):
    count, width = residual.shape
    groups = NX * NY
    parts = splits(width)
    return pl.pallas_call(
        reduce_kernel,
        out_shape=jax.ShapeDtypeStruct((count, width), jnp.bfloat16),
        in_specs=[pl.BlockSpec(memory_space=pltpu.VMEM)] * 2,
        out_specs=pl.BlockSpec(memory_space=pltpu.VMEM),
        scratch_shapes=[
            pltpu.VMEM((groups, count, parts[0][1]), jnp.bfloat16),
            pltpu.VMEM((groups, count, parts[1][1]), jnp.bfloat16),
            pltpu.VMEM((groups, count, parts[0][1]), jnp.bfloat16),
            pltpu.VMEM((groups, count, parts[1][1]), jnp.bfloat16),
            pltpu.SemaphoreType.DMA((2, groups)),
            pltpu.SemaphoreType.DMA((2, groups)),
        ],
        compiler_params=pltpu.CompilerParams(collective_id=1, has_side_effects=True),
    )(product.reshape(groups, count, width), residual)


def passed_along(block, axis, distance):
    devices = range(lax.axis_size(axis))
    route = [((i - distance) % len(devices), i) for i in devices]
    return lax.ppermute(block, axis, route)


def owner_ranks(owners):
    count_all = owners.shape[0]
    same_owner = owners[:, None] == owners[None, :]
    position = jnp.arange(count_all, dtype=jnp.int32)
    earlier = position[None, :] < position[:, None]
    return jnp.sum(jnp.where(same_owner & earlier, 1, 0), axis=1).astype(jnp.int32)


def slot_requests(owners, capacity, groups):
    slot_of = owners * capacity + owner_ranks(owners)
    slot_total = groups * capacity
    matches = slot_of[None, :] == jnp.arange(slot_total, dtype=jnp.int32)[:, None]
    request_ids = jnp.arange(owners.shape[0], dtype=jnp.int32)
    found_ids = jnp.sum(jnp.where(matches, request_ids[None, :] + 1, 0), axis=1)
    return found_ids - 1


def attend(queries, new_pairs, cached, lengths):
    slot_count = queries.shape[0]
    draft_steps = queries.shape[1]
    cached_len = cached.shape[1]
    pair_width = cached.shape[2] // 2
    key_span = cached_len + draft_steps
    key_rows = jnp.concatenate([cached[:, :, :pair_width], new_pairs[:, :, :pair_width]], axis=1)
    values = jnp.concatenate([cached[:, :, pair_width:], new_pairs[:, :, pair_width:]], axis=1)
    key_rows = key_rows.reshape(slot_count, key_span, KVH, HD)
    values = values.reshape(slot_count, key_span, KVH, HD)
    grouped = queries.reshape(slot_count, draft_steps, KVH, HEADS // KVH, HD)
    scores = jnp.einsum(
        "sjkgd,spkd->skgjp", grouped, key_rows, preferred_element_type=jnp.float32
    ) * HD ** (-0.5)
    position = jnp.arange(key_span, dtype=jnp.int32)
    step_ids = jnp.arange(draft_steps, dtype=jnp.int32)
    cached_ok = (position[None, :] < lengths[:, None]) & (position[None, :] < cached_len)
    fresh_ok = (position[None, :] >= cached_len) & (
        position[None, :] - cached_len <= step_ids[:, None]
    )
    allowed = cached_ok[:, None, :] | fresh_ok[None, :, :]
    scores = jnp.where(allowed[:, None, None, :, :], scores, -jnp.inf)
    row_max = jnp.max(scores, axis=-1, keepdims=True)
    weights = jnp.exp(scores - row_max)
    probabilities = (weights / jnp.sum(weights, axis=-1, keepdims=True)).astype(jnp.bfloat16)
    attended = jnp.einsum(
        "skgjp,spkd->sjkgd", probabilities, values, preferred_element_type=jnp.float32
    )
    return attended.reshape(slot_count, draft_steps, HEADS * HD).astype(jnp.bfloat16)


def on_device(
    hidden, norm_gain, w_query, w_keyval, w_out, kv_cache, owner_map, accepted, context, draft_ids
):
    groups = lax.axis_size("tp")
    my_index = lax.axis_index("tp")
    owners = owner_map[0]
    accepts = accepted[0]
    lengths = context[0]
    token_ids = draft_ids[0]
    requests = owners.shape[0]
    draft_steps = token_ids.shape[1]
    per_device = requests // groups
    capacity = kv_cache.shape[1]
    query_cols = w_query.shape[2]
    pair_cols = w_keyval.shape[1]
    row_width = query_cols + pair_cols
    weight_query = w_query[0]
    weight_pair = w_keyval[0]
    weight_out = w_out[0]
    cached = kv_cache[0]
    rows_f32 = hidden[0].astype(jnp.float32)
    inverse_rms = lax.rsqrt(jnp.mean(rows_f32 * rows_f32, axis=1, keepdims=True) + epsilon)
    normed = (rows_f32 * inverse_rms * norm_gain[0][None, :]).astype(jnp.bfloat16)
    slot_of = owners * capacity + owner_ranks(owners)
    holders = slot_requests(owners, capacity, groups)
    safe_req = jnp.maximum(holders, 0)
    my_slots = lax.dynamic_slice_in_dim(holders, my_index * capacity, capacity)
    my_live = my_slots >= 0
    my_safe = jnp.maximum(my_slots, 0)
    step_ids = jnp.arange(draft_steps, dtype=jnp.int32)
    blocks = 1
    per_block = per_device // blocks
    kept_pairs = jnp.zeros((capacity, draft_steps, groups * pair_cols), jnp.bfloat16)
    row_piece = gather_rows(normed)
    query_part = jnp.dot(row_piece, weight_query, preferred_element_type=jnp.float32).astype(
        jnp.bfloat16
    )
    pair_part = lax.dot_general(
        row_piece, weight_pair, (((1,), (1,)), ((), ())), preferred_element_type=jnp.float32
    ).astype(jnp.bfloat16)
    projected = jnp.concatenate([query_part, pair_part], axis=1)
    in_block = (holders >= 0) & (safe_req % per_device // per_block == 0)
    source_row = safe_req // per_device * per_block + (safe_req % per_device - 0)
    slot_flags = jnp.repeat(in_block, draft_steps)
    source = (source_row[:, None] * draft_steps + step_ids[None, :]).reshape(-1)
    source = jnp.where(slot_flags, source, 0)
    outgoing = jnp.take(projected, source, axis=0)
    outgoing = jnp.where(slot_flags[:, None], outgoing, jnp.zeros_like(outgoing))
    arrived = lax.all_to_all(outgoing, "tp", split_axis=0, concat_axis=1, tiled=True)
    arrived = arrived.reshape(capacity, draft_steps, groups, row_width)
    queries = arrived[:, :, :, :query_cols].reshape(capacity, draft_steps, groups * query_cols)
    new_pairs = arrived[:, :, :, query_cols:].reshape(capacity, draft_steps, groups * pair_cols)
    mine_block = my_live & (my_safe % per_device // per_block == 0)
    slot_lengths = jnp.where(mine_block, jnp.take(lengths, my_safe), 0)
    attended = attend(queries, new_pairs, cached, slot_lengths)
    flat_heads = attended.reshape(capacity * draft_steps, groups * query_cols)
    returned = lax.all_to_all(flat_heads, "tp", split_axis=1, concat_axis=0, tiled=True)
    block_requests = (
        jnp.arange(groups, dtype=jnp.int32)[:, None] * per_device
        + 0
        + jnp.arange(per_block, dtype=jnp.int32)[None, :]
    ).reshape(-1)
    target = (jnp.take(slot_of, block_requests)[:, None] * draft_steps + step_ids[None, :]).reshape(
        -1
    )
    heads_block = jnp.take(returned, target, axis=0)
    product = jnp.dot(heads_block, weight_out, preferred_element_type=jnp.float32).astype(
        jnp.bfloat16
    )
    results = reduce_rows(product, hidden[0])
    accept_now = mine_block[:, None] & (step_ids[None, :] < jnp.take(accepts, my_safe)[:, None])
    kept_pairs = jnp.where(accept_now[:, :, None], new_pairs, kept_pairs)
    shifted = passed_along(results, "section", 1)
    accept_all = my_live[:, None] & (step_ids[None, :] < jnp.take(accepts, my_safe)[:, None])
    kept_ids = jnp.where(accept_all, jnp.take(token_ids, my_safe, axis=0), -1).reshape(-1)
    committed = kept_pairs.reshape(capacity * draft_steps, groups * pair_cols)
    return (shifted[None], committed[None], kept_ids[None])


def solution(mesh):
    placed = (
        P("section", "tp", None),
        P("section", None),
        P("section", None, "tp"),
        P("section", "tp", None),
        P("section", "tp", None),
        P("section", "tp", None, None),
        P("section", None),
        P("section", None),
        P("section", None),
        P("section", None, None),
    )
    return jax.shard_map(
        on_device,
        mesh=mesh,
        in_specs=placed,
        out_specs=(P("section", "tp", None), P("section", "tp", None), P("section", "tp")),
        check_vma=False,
    )
```

```python
import jax
import jax.numpy as jnp
from jax import lax
from jax.experimental import pallas as pl
from jax.experimental.pallas import tpu as pltpu
from jax.sharding import PartitionSpec as P

HEADS = 32
KVH = 4
HD = 128


epsilon = 1e-06


NX = 4
NY = 8
LANES = 128
XY_SHARE = 26 / 64


def splits(width):
    first = max(1, round(width // LANES * XY_SHARE)) * LANES
    return ((0, first), (first, width - first))


def far_positive(mode, axis, dx, dy):
    if mode == 0:
        return True if axis == 0 else dx % 2 == 0
    return dy % 2 == 0 if axis == 0 else False


def reach(mode, axis, sign, dx, dy):
    half = (NX if axis == 0 else NY) // 2
    return half if far_positive(mode, axis, dx, dy) == (sign > 0) else half - 1


def travelled(mode, axis, dx, dy):
    size = NX if axis == 0 else NY
    ahead = (-dx if axis == 0 else -dy) % size
    if ahead == 0:
        return 0
    if ahead <= reach(mode, axis, 1, dx, dy):
        return ahead
    return ahead - size


def children(mode, dx, dy):
    first, second = (0, 1) if mode == 0 else (1, 0)
    hops = []
    step1 = travelled(mode, first, dx, dy)
    step2 = travelled(mode, second, dx, dy)
    if step2 == 0:
        for sign in (1, -1):
            if step1 * sign >= 0 and abs(step1) < reach(mode, first, sign, dx, dy):
                hops.append((first, sign))
    for sign in (1, -1):
        if step2 * sign >= 0 and abs(step2) < reach(mode, second, sign, dx, dy):
            hops.append((second, sign))
    return hops


def moved(axis, sign, dx, dy):
    return ((dx - sign) % NX, dy) if axis == 0 else (dx, (dy - sign) % NY)


def parent(mode, dx, dy):
    first, second = (0, 1) if mode == 0 else (1, 0)
    step2 = travelled(mode, second, dx, dy)
    axis = second if step2 else first
    return (axis, 1 if travelled(mode, axis, dx, dy) > 0 else -1)


def arrival_order(weights):
    free = {}
    order = []
    pending = [(0.0, 0, 0, 0), (0.0, 1, 0, 0)]
    while pending:
        pending.sort()
        now, mode, dx, dy = pending.pop(0)
        order.append((mode, dx, dy))
        for axis, sign in children(mode, dx, dy):
            begin = max(now, free.get((axis, sign), 0.0))
            free[axis, sign] = begin + weights[mode]
            pending.append((begin + weights[mode] + 1.6, mode) + moved(axis, sign, dx, dy))
    return order


def place_of(dx, dy):
    return dx * NY + dy


def neighbours(mx, my):
    return {
        (0, 1): lax.rem(mx + 1, NX) * NY + my,
        (0, -1): lax.rem(mx + NX - 1, NX) * NY + my,
        (1, 1): mx * NY + lax.rem(my + 1, NY),
        (1, -1): mx * NY + lax.rem(my + NY - 1, NY),
    }


def greet(devices):
    barrier = pltpu.get_barrier_semaphore()
    for device in devices:
        pl.semaphore_signal(
            barrier, inc=1, device_id={"tp": device}, device_id_type=pl.DeviceIdType.MESH
        )
    pl.semaphore_wait(barrier, len(devices))


def block_at(mx, my, dx, dy):
    return lax.rem(mx + dx, NX) * NY + lax.rem(my + dy, NY)


def slot_matrix(slot_ref, rows):
    row = lax.broadcasted_iota(jnp.int32, (rows, slot_ref.shape[1]), 0)
    return jnp.where(row == slot_ref[...], 1.0, 0.0).astype(jnp.bfloat16)


def project_kernel(
    hid_ref, gain_ref, slot_ref, wq_hbm, wp_hbm, out_ref,
    x_ref, all_ref, wq_ref, wp_ref, acc_ref, load_sems, send_sems, recv_sems,
):
    me = lax.axis_index("tp")
    mx = me // NY
    my = lax.rem(me, NY)
    near = neighbours(mx, my)
    width = hid_ref.shape[1]
    parts = splits(width)
    loads = [
        pltpu.make_async_copy(wq_hbm, wq_ref, load_sems.at[0]),
        pltpu.make_async_copy(wp_hbm, wp_ref, load_sems.at[1]),
    ]
    for load in loads:
        load.start()
    rows = hid_ref[...].astype(jnp.float32)
    inverse_rms = lax.rsqrt(jnp.mean(rows * rows, axis=1, keepdims=True) + epsilon)
    x_ref[...] = (rows * inverse_rms * gain_ref[...]).astype(jnp.bfloat16)
    greet(list(near.values()))

    def copy(mode, dx, dy, link):
        start, size = parts[mode]
        there = place_of(*moved(*link, dx, dy))
        cols = pl.ds(start, size)
        block = block_at(mx, my, dx, dy)
        source = x_ref.at[:, cols] if (dx, dy) == (0, 0) else all_ref.at[block, :, cols]
        return pltpu.make_async_remote_copy(
            src_ref=source,
            dst_ref=all_ref.at[block, :, cols],
            send_sem=send_sems.at[mode, there],
            recv_sem=recv_sems.at[mode, there],
            device_id={"tp": near[link]},
            device_id_type=pl.DeviceIdType.MESH,
        )

    started = []
    order = arrival_order([part[1] * 16 / 46e3 for part in parts])
    for mode, dx, dy in order:
        if (dx, dy) != (0, 0):
            start, size = parts[mode]
            landed = all_ref.at[block_at(mx, my, dx, dy), :, pl.ds(start, size)]
            pltpu.make_async_remote_copy(
                src_ref=landed,
                dst_ref=landed,
                send_sem=send_sems.at[mode, place_of(dx, dy)],
                recv_sem=recv_sems.at[mode, place_of(dx, dy)],
                device_id={"tp": near[parent(mode, dx, dy)]},
                device_id_type=pl.DeviceIdType.MESH,
            ).wait_recv()
        for link in children(mode, dx, dy):
            sent = copy(mode, dx, dy, link)
            sent.start()
            started.append(sent)
        if len(started) == 8:
            all_ref[me] = x_ref[...]
            for load in loads:
                load.wait()
    groups, count = all_ref.shape[:2]
    tokens = groups * count
    query_cols = wq_ref.shape[1]
    pair_cols = wp_ref.shape[0]
    step = width // 8
    acc_ref[...] = jnp.zeros_like(acc_ref)

    def add(k, carry):
        cols = pl.ds(pl.multiple_of(k * step, step), step)
        x = all_ref[:, :, cols].reshape(tokens, step)
        acc_ref[:, :query_cols] += jnp.dot(
            x, wq_ref[cols, :], preferred_element_type=jnp.float32
        )
        acc_ref[:, query_cols:] += lax.dot_general(
            x, wp_ref[:, cols], (((1,), (1,)), ((), ())), preferred_element_type=jnp.float32
        )
        return carry

    lax.fori_loop(0, 8, add, 0)
    queries = acc_ref[:, :query_cols].astype(jnp.bfloat16)
    pairs = acc_ref[:, query_cols:].astype(jnp.bfloat16)
    lane = lax.broadcasted_iota(jnp.int32, (pair_cols, LANES), 1)
    source = lax.broadcasted_iota(jnp.int32, (pair_cols, LANES), 0)
    offset = lax.rem(me, LANES // pair_cols) * pair_cols
    spread = jnp.where(lane == source + offset, 1.0, 0.0).astype(jnp.bfloat16)
    placed = jnp.dot(pairs, spread, preferred_element_type=jnp.float32).astype(jnp.bfloat16)
    chosen = slot_matrix(slot_ref, out_ref.shape[0] * out_ref.shape[1])
    out_shape = out_ref.shape[:2] + (LANES,)
    out_ref[:, :, :LANES] = (
        jnp.dot(chosen, queries, preferred_element_type=jnp.float32)
        .reshape(out_shape).astype(jnp.bfloat16)
    )
    out_ref[:, :, LANES:] = (
        jnp.dot(chosen, placed, preferred_element_type=jnp.float32)
        .reshape(out_shape).astype(jnp.bfloat16)
    )
    for sent in started:
        sent.wait_send()


def project_rows(hidden, gain, slot_tokens, weight_query, weight_pair, slot_rows):
    count, width = hidden.shape
    groups = NX * NY
    vmem = pl.BlockSpec(memory_space=pltpu.VMEM)
    hbm = pl.BlockSpec(memory_space=pl.ANY)
    query_cols = weight_query.shape[1]
    pair_cols = weight_pair.shape[0]
    return pl.pallas_call(
        project_kernel,
        out_shape=jax.ShapeDtypeStruct((groups, slot_rows, 2 * LANES), jnp.bfloat16),
        in_specs=[vmem, vmem, vmem, hbm, hbm],
        out_specs=vmem,
        scratch_shapes=[
            pltpu.VMEM((count, width), jnp.bfloat16),
            pltpu.VMEM((groups, count, width), jnp.bfloat16),
            pltpu.VMEM(weight_query.shape, jnp.bfloat16),
            pltpu.VMEM(weight_pair.shape, jnp.bfloat16),
            pltpu.VMEM((groups * count, query_cols + pair_cols), jnp.float32),
            pltpu.SemaphoreType.DMA((2,)),
            pltpu.SemaphoreType.DMA((2, groups)),
            pltpu.SemaphoreType.DMA((2, groups)),
        ],
        compiler_params=pltpu.CompilerParams(collective_id=0, has_side_effects=True),
    )(hidden, gain, slot_tokens, weight_query, weight_pair)


def attend_kernel(len_ref, got_ref, cache_ref, out_ref, pairs_ref):
    slot_rows = got_ref.shape[1]
    slots = len_ref.shape[0]
    steps = slot_rows // slots
    cached_rows = cache_ref.shape[0]
    cached_len = cached_rows // slots
    span = cached_rows + slot_rows
    per_kv = HEADS // KVH
    rows = per_kv * slot_rows
    row = lax.rem(lax.broadcasted_iota(jnp.int32, (rows, span), 0), slot_rows)
    col = lax.broadcasted_iota(jnp.int32, (rows, span), 1)
    fresh = col - cached_rows
    allowed = (fresh >= 0) & (fresh // steps == row // steps) & (fresh <= row)
    for slot in range(slots):
        base = slot * cached_len
        allowed |= (row // steps == slot) & (col >= base) & (col < base + len_ref[slot])
    pieces = got_ref.shape[0] // (2 * KVH)
    for e in range(KVH):
        cols = slice(e * HD, (e + 1) * HD)
        value_cols = slice((KVH + e) * HD, (KVH + e + 1) * HD)

        def joined(first):
            total = got_ref[first, :, LANES:].astype(jnp.float32)
            for i in range(1, pieces):
                total = total + got_ref[first + i, :, LANES:].astype(jnp.float32)
            return total.astype(jnp.bfloat16)

        new_keys = joined(e * pieces)
        new_values = joined((KVH + e) * pieces)
        pairs_ref[:, cols] = new_keys
        pairs_ref[:, value_cols] = new_values
        keys = jnp.concatenate([cache_ref[:, cols], new_keys], axis=0)
        values = jnp.concatenate([cache_ref[:, value_cols], new_values], axis=0)
        queries = got_ref[e * per_kv : (e + 1) * per_kv, :, :LANES].reshape(rows, HD)
        scores = lax.dot_general(
            queries, keys, (((1,), (1,)), ((), ())), preferred_element_type=jnp.float32
        ) * HD ** (-0.5)
        scores = jnp.where(allowed, scores, -jnp.inf)
        weights = jnp.exp(scores - jnp.max(scores, axis=1, keepdims=True))
        probs = (weights / jnp.sum(weights, axis=1, keepdims=True)).astype(jnp.bfloat16)
        attended = jnp.dot(probs, values, preferred_element_type=jnp.float32)
        out_ref[e * per_kv : (e + 1) * per_kv] = attended.reshape(
            per_kv, slot_rows, HD
        ).astype(jnp.bfloat16)


def attend_slots(lengths, arrived, cached):
    groups, slot_rows, _ = arrived.shape
    slots, cached_len, width = cached.shape
    vmem = pl.BlockSpec(memory_space=pltpu.VMEM)
    return pl.pallas_call(
        attend_kernel,
        out_shape=(
            jax.ShapeDtypeStruct((groups, slot_rows, HD), jnp.bfloat16),
            jax.ShapeDtypeStruct((slot_rows, width), jnp.bfloat16),
        ),
        in_specs=[pl.BlockSpec(memory_space=pltpu.SMEM), vmem, vmem],
        out_specs=(vmem, vmem),
    )(lengths, arrived, cached.reshape(slots * cached_len, width))


def reduce_kernel(
    slot_ref, heads_ref, hid_ref, wo_hbm, out_ref,
    p_ref, wo_ref, res_ref, got0, got1, stage0, stage1,
    load_sem, shift_send, shift_recv, send_sems, recv_sems,
):
    me = lax.axis_index("tp")
    section = lax.axis_index("section")
    sections = lax.axis_size("section")
    after = lax.rem(section + 1, sections)
    before = lax.rem(section + sections - 1, sections)
    mx = me // NY
    my = lax.rem(me, NY)
    near = neighbours(mx, my)
    width = hid_ref.shape[1]
    parts = splits(width)
    got = (got0, got1)
    stage = (stage0, stage1)
    load = pltpu.make_async_copy(wo_hbm, wo_ref, load_sem)
    load.start()
    barrier = pltpu.get_barrier_semaphore()
    for device in near.values():
        pl.semaphore_signal(
            barrier, inc=1, device_id={"tp": device}, device_id_type=pl.DeviceIdType.MESH
        )
    pl.semaphore_signal(
        barrier, inc=1, device_id={"section": before}, device_id_type=pl.DeviceIdType.MESH
    )
    groups, count = p_ref.shape[:2]
    tokens = groups * count
    slot_rows = heads_ref.shape[0] * heads_ref.shape[1]
    chosen = slot_matrix(slot_ref, slot_rows)
    heads = lax.dot_general(
        chosen, heads_ref[...].reshape(slot_rows, heads_ref.shape[2]),
        (((0,), (0,)), ((), ())), preferred_element_type=jnp.float32,
    ).astype(jnp.bfloat16)
    load.wait()
    step = 256

    def multiply(mode):
        start, size = parts[mode]

        def one(k, carry):
            cols = pl.ds(pl.multiple_of(start + k * step, LANES), step)
            piece = jnp.dot(heads, wo_ref[:, cols], preferred_element_type=jnp.float32)
            p_ref[:, :, cols] = piece.reshape(groups, count, step).astype(jnp.bfloat16)
            return carry

        lax.fori_loop(0, size // step, one, 0)

    started = []

    def total(mode, dx, dy):
        start, size = parts[mode]
        block = block_at(mx, my, dx, dy)
        summed = p_ref[block, :, pl.ds(start, size)].astype(jnp.float32)
        for link in children(mode, dx, dy):
            slot = place_of(*moved(*link, dx, dy))
            pltpu.make_async_remote_copy(
                src_ref=stage[mode].at[slot],
                dst_ref=got[mode].at[slot],
                send_sem=send_sems.at[mode, slot],
                recv_sem=recv_sems.at[mode, slot],
                device_id={"tp": near[link]},
                device_id_type=pl.DeviceIdType.MESH,
            ).wait_recv()
            summed = summed + got[mode][slot].astype(jnp.float32)
        return summed

    def send(mode, dx, dy, source):
        slot = place_of(dx, dy)
        axis, sign = parent(mode, dx, dy)
        sent = pltpu.make_async_remote_copy(
            src_ref=source,
            dst_ref=got[mode].at[slot],
            send_sem=send_sems.at[mode, slot],
            recv_sem=recv_sems.at[mode, slot],
            device_id={"tp": near[axis, -sign]},
            device_id_type=pl.DeviceIdType.MESH,
        )
        sent.start()
        started.append(sent)

    def send_leaf(mode, dx, dy):
        start, size = parts[mode]
        send(mode, dx, dy, p_ref.at[block_at(mx, my, dx, dy), :, pl.ds(start, size)])

    def shift(mode):
        start, size = parts[mode]
        cols = pl.ds(start, size)
        return pltpu.make_async_remote_copy(
            src_ref=res_ref.at[:, cols],
            dst_ref=out_ref.at[:, cols],
            send_sem=shift_send.at[mode],
            recv_sem=shift_recv.at[mode],
            device_id={"section": after},
            device_id_type=pl.DeviceIdType.MESH,
        )

    order = arrival_order([part[1] * 16 / 46e3 for part in parts])[::-1]
    multiply(1)
    pl.semaphore_wait(barrier, len(near) + 1)
    early = [event for event in order[:16] if event[0] == 1 and not children(*event)]
    for event in early:
        send_leaf(*event)
    multiply(0)
    for event in order:
        if event in early:
            continue
        mode, dx, dy = event
        start, size = parts[mode]
        if (dx, dy) == (0, 0):
            cols = pl.ds(start, size)
            summed = total(mode, dx, dy) + hid_ref[:, cols].astype(jnp.float32)
            res_ref[:, cols] = summed.astype(jnp.bfloat16)
            shift(mode).start()
        elif children(mode, dx, dy):
            slot = place_of(dx, dy)
            stage[mode][slot] = total(mode, dx, dy).astype(jnp.bfloat16)
            send(mode, dx, dy, stage[mode].at[slot])
        else:
            send_leaf(mode, dx, dy)
    for sent in started:
        sent.wait_send()
    for mode in (0, 1):
        shift(mode).wait()


def reduce_rows(slot_tokens, heads, residual, weight_out):
    count, width = residual.shape
    groups = NX * NY
    parts = splits(width)
    vmem = pl.BlockSpec(memory_space=pltpu.VMEM)
    return pl.pallas_call(
        reduce_kernel,
        out_shape=jax.ShapeDtypeStruct((count, width), jnp.bfloat16),
        in_specs=[vmem, vmem, vmem, pl.BlockSpec(memory_space=pl.ANY)],
        out_specs=vmem,
        scratch_shapes=[
            pltpu.VMEM((groups, count, width), jnp.bfloat16),
            pltpu.VMEM(weight_out.shape, jnp.bfloat16),
            pltpu.VMEM((count, width), jnp.bfloat16),
            pltpu.VMEM((groups, count, parts[0][1]), jnp.bfloat16),
            pltpu.VMEM((groups, count, parts[1][1]), jnp.bfloat16),
            pltpu.VMEM((groups, count, parts[0][1]), jnp.bfloat16),
            pltpu.VMEM((groups, count, parts[1][1]), jnp.bfloat16),
            pltpu.SemaphoreType.DMA,
            pltpu.SemaphoreType.DMA((2,)),
            pltpu.SemaphoreType.DMA((2,)),
            pltpu.SemaphoreType.DMA((2, groups)),
            pltpu.SemaphoreType.DMA((2, groups)),
        ],
        compiler_params=pltpu.CompilerParams(collective_id=1, has_side_effects=True),
    )(slot_tokens, heads, residual, weight_out)


def owner_ranks(owners):
    count_all = owners.shape[0]
    same_owner = owners[:, None] == owners[None, :]
    position = jnp.arange(count_all, dtype=jnp.int32)
    earlier = position[None, :] < position[:, None]
    return jnp.sum(jnp.where(same_owner & earlier, 1, 0), axis=1).astype(jnp.int32)


def on_device(
    hidden, norm_gain, w_query, w_keyval, w_out, kv_cache, owner_map, accepted, context, draft_ids
):
    my_index = lax.axis_index("tp")
    owners = owner_map[0]
    accepts = accepted[0]
    lengths = context[0]
    token_ids = draft_ids[0]
    draft_steps = token_ids.shape[1]
    capacity = kv_cache.shape[1]
    slot_rows = capacity * draft_steps
    slot_of = owners * capacity + owner_ranks(owners)
    step_ids = jnp.arange(draft_steps, dtype=jnp.int32)
    slot_tokens = (slot_of[:, None] * draft_steps + step_ids[None, :]).reshape(1, -1)
    my_slots = my_index * capacity + jnp.arange(capacity, dtype=jnp.int32)
    mine = my_slots[:, None] == slot_of[None, :]
    my_lengths = jnp.sum(jnp.where(mine, lengths[None, :], 0), axis=1)
    my_accepts = jnp.sum(jnp.where(mine, accepts[None, :], 0), axis=1)
    my_ids = jnp.sum(jnp.where(mine[:, :, None], token_ids[None, :, :], 0), axis=1)
    outgoing = project_rows(
        hidden[0], norm_gain, slot_tokens, w_query[0], w_keyval[0], slot_rows
    )
    arrived = lax.all_to_all(outgoing, "tp", split_axis=0, concat_axis=0, tiled=True)
    attended, new_pairs = attend_slots(my_lengths, arrived, kv_cache[0])
    returned = lax.all_to_all(attended, "tp", split_axis=0, concat_axis=0, tiled=True)
    shifted = reduce_rows(slot_tokens, returned, hidden[0], w_out[0])
    keep = step_ids[None, :] < my_accepts[:, None]
    kept_ids = jnp.where(keep, my_ids, -1).reshape(-1)
    committed = jnp.where(keep.reshape(-1)[:, None], new_pairs, jnp.zeros_like(new_pairs))
    return (shifted[None], committed[None], kept_ids[None])


def solution(mesh):
    placed = (
        P("section", "tp", None),
        P("section", None),
        P("section", None, "tp"),
        P("section", "tp", None),
        P("section", "tp", None),
        P("section", "tp", None, None),
        P("section", None),
        P("section", None),
        P("section", None),
        P("section", None, None),
    )
    return jax.shard_map(
        on_device,
        mesh=mesh,
        in_specs=placed,
        out_specs=(P("section", "tp", None), P("section", "tp", None), P("section", "tp")),
        check_vma=False,
    )
```

```python
import jax
import jax.numpy as jnp
from jax import lax
from jax.experimental import pallas as pl
from jax.experimental.pallas import tpu as pltpu
from jax.sharding import PartitionSpec as P

HEADS = 32
KVH = 4
HD = 128


epsilon = 1e-06


NX = 4
NY = 8
LANES = 128
XY_SHARE = 26 / 64


def splits(width):
    first = max(1, round(width // LANES * XY_SHARE)) * LANES
    return ((0, first), (first, width - first))


def far_positive(mode, axis, dx, dy):
    if mode == 0:
        return True if axis == 0 else dx % 2 == 0
    return dy % 2 == 0 if axis == 0 else False


def reach(mode, axis, sign, dx, dy):
    half = (NX if axis == 0 else NY) // 2
    return half if far_positive(mode, axis, dx, dy) == (sign > 0) else half - 1


def travelled(mode, axis, dx, dy):
    size = NX if axis == 0 else NY
    ahead = (-dx if axis == 0 else -dy) % size
    if ahead == 0:
        return 0
    if ahead <= reach(mode, axis, 1, dx, dy):
        return ahead
    return ahead - size


def children(mode, dx, dy):
    first, second = (0, 1) if mode == 0 else (1, 0)
    hops = []
    step1 = travelled(mode, first, dx, dy)
    step2 = travelled(mode, second, dx, dy)
    if step2 == 0:
        for sign in (1, -1):
            if step1 * sign >= 0 and abs(step1) < reach(mode, first, sign, dx, dy):
                hops.append((first, sign))
    for sign in (1, -1):
        if step2 * sign >= 0 and abs(step2) < reach(mode, second, sign, dx, dy):
            hops.append((second, sign))
    return hops


def moved(axis, sign, dx, dy):
    return ((dx - sign) % NX, dy) if axis == 0 else (dx, (dy - sign) % NY)


def parent(mode, dx, dy):
    first, second = (0, 1) if mode == 0 else (1, 0)
    step2 = travelled(mode, second, dx, dy)
    axis = second if step2 else first
    return (axis, 1 if travelled(mode, axis, dx, dy) > 0 else -1)


def arrival_order(weights):
    free = {}
    order = []
    pending = [(0.0, 0, 0, 0), (0.0, 1, 0, 0)]
    while pending:
        pending.sort()
        now, mode, dx, dy = pending.pop(0)
        order.append((mode, dx, dy))
        for axis, sign in children(mode, dx, dy):
            begin = max(now, free.get((axis, sign), 0.0))
            free[axis, sign] = begin + weights[mode]
            pending.append((begin + weights[mode] + 1.6, mode) + moved(axis, sign, dx, dy))
    return order


def place_of(dx, dy):
    return dx * NY + dy


def neighbours(mx, my):
    return {
        (0, 1): lax.rem(mx + 1, NX) * NY + my,
        (0, -1): lax.rem(mx + NX - 1, NX) * NY + my,
        (1, 1): mx * NY + lax.rem(my + 1, NY),
        (1, -1): mx * NY + lax.rem(my + NY - 1, NY),
    }


def greet(devices):
    barrier = pltpu.get_barrier_semaphore()
    for device in devices:
        pl.semaphore_signal(
            barrier, inc=1, device_id={"tp": device}, device_id_type=pl.DeviceIdType.MESH
        )
    pl.semaphore_wait(barrier, len(devices))


def block_at(mx, my, dx, dy):
    return lax.rem(mx + dx, NX) * NY + lax.rem(my + dy, NY)


def slot_matrix(slot_ref, rows):
    row = lax.broadcasted_iota(jnp.int32, (rows, slot_ref.shape[1]), 0)
    return jnp.where(row == slot_ref[...], 1.0, 0.0).astype(jnp.bfloat16)


def project_kernel(
    hid_ref, gain_ref, slot_ref, wq_hbm, wp_hbm, out_ref,
    x_ref, all_ref, wq_ref, wp_ref, acc_ref, load_sems, send_sems, recv_sems,
):
    me = lax.axis_index("tp")
    mx = me // NY
    my = lax.rem(me, NY)
    near = neighbours(mx, my)
    width = hid_ref.shape[1]
    parts = splits(width)
    loads = [
        pltpu.make_async_copy(wq_hbm, wq_ref, load_sems.at[0]),
        pltpu.make_async_copy(wp_hbm, wp_ref, load_sems.at[1]),
    ]
    for load in loads:
        load.start()
    rows = hid_ref[...].astype(jnp.float32)
    inverse_rms = lax.rsqrt(jnp.mean(rows * rows, axis=1, keepdims=True) + epsilon)
    x_ref[...] = (rows * inverse_rms * gain_ref[...]).astype(jnp.bfloat16)
    greet(list(near.values()))

    def copy(mode, dx, dy, link):
        start, size = parts[mode]
        there = place_of(*moved(*link, dx, dy))
        cols = pl.ds(start, size)
        block = block_at(mx, my, dx, dy)
        source = x_ref.at[:, cols] if (dx, dy) == (0, 0) else all_ref.at[block, :, cols]
        return pltpu.make_async_remote_copy(
            src_ref=source,
            dst_ref=all_ref.at[block, :, cols],
            send_sem=send_sems.at[mode, there],
            recv_sem=recv_sems.at[mode, there],
            device_id={"tp": near[link]},
            device_id_type=pl.DeviceIdType.MESH,
        )

    started = []
    order = arrival_order([part[1] * 16 / 46e3 for part in parts])
    for mode, dx, dy in order:
        if (dx, dy) != (0, 0):
            start, size = parts[mode]
            landed = all_ref.at[block_at(mx, my, dx, dy), :, pl.ds(start, size)]
            pltpu.make_async_remote_copy(
                src_ref=landed,
                dst_ref=landed,
                send_sem=send_sems.at[mode, place_of(dx, dy)],
                recv_sem=recv_sems.at[mode, place_of(dx, dy)],
                device_id={"tp": near[parent(mode, dx, dy)]},
                device_id_type=pl.DeviceIdType.MESH,
            ).wait_recv()
        for link in children(mode, dx, dy):
            sent = copy(mode, dx, dy, link)
            sent.start()
            started.append(sent)
        if len(started) == 8:
            all_ref[me] = x_ref[...]
            for load in loads:
                load.wait()
    groups, count = all_ref.shape[:2]
    tokens = groups * count
    query_cols = wq_ref.shape[1]
    pair_cols = wp_ref.shape[0]
    step = width // 8
    acc_ref[...] = jnp.zeros_like(acc_ref)

    def add(k, carry):
        cols = pl.ds(pl.multiple_of(k * step, step), step)
        x = all_ref[:, :, cols].reshape(tokens, step)
        acc_ref[:, :query_cols] += jnp.dot(
            x, wq_ref[cols, :], preferred_element_type=jnp.float32
        )
        acc_ref[:, query_cols:] += lax.dot_general(
            x, wp_ref[:, cols], (((1,), (1,)), ((), ())), preferred_element_type=jnp.float32
        )
        return carry

    lax.fori_loop(0, 8, add, 0)
    queries = acc_ref[:, :query_cols].astype(jnp.bfloat16)
    pairs = acc_ref[:, query_cols:].astype(jnp.bfloat16)
    lane = lax.broadcasted_iota(jnp.int32, (pair_cols, LANES), 1)
    source = lax.broadcasted_iota(jnp.int32, (pair_cols, LANES), 0)
    offset = lax.rem(me, LANES // pair_cols) * pair_cols
    spread = jnp.where(lane == source + offset, 1.0, 0.0).astype(jnp.bfloat16)
    placed = jnp.dot(pairs, spread, preferred_element_type=jnp.float32).astype(jnp.bfloat16)
    chosen = slot_matrix(slot_ref, out_ref.shape[0] * out_ref.shape[1])
    out_shape = out_ref.shape[:2] + (LANES,)
    out_ref[:, :, :LANES] = (
        jnp.dot(chosen, queries, preferred_element_type=jnp.float32)
        .reshape(out_shape).astype(jnp.bfloat16)
    )
    out_ref[:, :, LANES:] = (
        jnp.dot(chosen, placed, preferred_element_type=jnp.float32)
        .reshape(out_shape).astype(jnp.bfloat16)
    )
    for sent in started:
        sent.wait_send()


def project_rows(hidden, gain, slot_tokens, weight_query, weight_pair, slot_rows):
    count, width = hidden.shape
    groups = NX * NY
    vmem = pl.BlockSpec(memory_space=pltpu.VMEM)
    hbm = pl.BlockSpec(memory_space=pl.ANY)
    query_cols = weight_query.shape[1]
    pair_cols = weight_pair.shape[0]
    return pl.pallas_call(
        project_kernel,
        out_shape=jax.ShapeDtypeStruct((groups, slot_rows, 2 * LANES), jnp.bfloat16),
        in_specs=[vmem, vmem, vmem, hbm, hbm],
        out_specs=vmem,
        scratch_shapes=[
            pltpu.VMEM((count, width), jnp.bfloat16),
            pltpu.VMEM((groups, count, width), jnp.bfloat16),
            pltpu.VMEM(weight_query.shape, jnp.bfloat16),
            pltpu.VMEM(weight_pair.shape, jnp.bfloat16),
            pltpu.VMEM((groups * count, query_cols + pair_cols), jnp.float32),
            pltpu.SemaphoreType.DMA((2,)),
            pltpu.SemaphoreType.DMA((2, groups)),
            pltpu.SemaphoreType.DMA((2, groups)),
        ],
        compiler_params=pltpu.CompilerParams(collective_id=0, has_side_effects=True),
    )(hidden, gain, slot_tokens, weight_query, weight_pair)


def attend_kernel(len_ref, got_ref, cache_ref, out_ref, pairs_ref):
    slot_rows = got_ref.shape[1]
    slots = len_ref.shape[0]
    steps = slot_rows // slots
    cached_rows = cache_ref.shape[0]
    cached_len = cached_rows // slots
    span = cached_rows + slot_rows
    per_kv = HEADS // KVH
    rows = per_kv * slot_rows
    row = lax.rem(lax.broadcasted_iota(jnp.int32, (rows, span), 0), slot_rows)
    col = lax.broadcasted_iota(jnp.int32, (rows, span), 1)
    fresh = col - cached_rows
    allowed = (fresh >= 0) & (fresh // steps == row // steps) & (fresh <= row)
    for slot in range(slots):
        base = slot * cached_len
        allowed |= (row // steps == slot) & (col >= base) & (col < base + len_ref[slot])
    pieces = got_ref.shape[0] // (2 * KVH)
    for e in range(KVH):
        cols = slice(e * HD, (e + 1) * HD)
        value_cols = slice((KVH + e) * HD, (KVH + e + 1) * HD)

        def joined(first):
            total = got_ref[first, :, LANES:].astype(jnp.float32)
            for i in range(1, pieces):
                total = total + got_ref[first + i, :, LANES:].astype(jnp.float32)
            return total.astype(jnp.bfloat16)

        new_keys = joined(e * pieces)
        new_values = joined((KVH + e) * pieces)
        pairs_ref[:, cols] = new_keys
        pairs_ref[:, value_cols] = new_values
        keys = jnp.concatenate([cache_ref[:, cols], new_keys], axis=0)
        values = jnp.concatenate([cache_ref[:, value_cols], new_values], axis=0)
        queries = got_ref[e * per_kv : (e + 1) * per_kv, :, :LANES].reshape(rows, HD)
        scores = lax.dot_general(
            queries, keys, (((1,), (1,)), ((), ())), preferred_element_type=jnp.float32
        ) * HD ** (-0.5)
        scores = jnp.where(allowed, scores, -jnp.inf)
        weights = jnp.exp(scores - jnp.max(scores, axis=1, keepdims=True))
        probs = (weights / jnp.sum(weights, axis=1, keepdims=True)).astype(jnp.bfloat16)
        attended = jnp.dot(probs, values, preferred_element_type=jnp.float32)
        out_ref[e * per_kv : (e + 1) * per_kv] = attended.reshape(
            per_kv, slot_rows, HD
        ).astype(jnp.bfloat16)


def exchange_kernel(
    len_ref, sent_ref, cache_ref, back_ref, pairs_ref,
    got_ref, att_ref, send0, recv0, send1, recv1,
):
    me = lax.axis_index("tp")
    groups = sent_ref.shape[0]
    barrier = pltpu.get_barrier_semaphore()

    def greet_one(i, carry):
        pl.semaphore_signal(
            barrier, inc=1, device_id={"tp": lax.rem(me + i, groups)},
            device_id_type=pl.DeviceIdType.MESH,
        )
        return carry

    lax.fori_loop(1, groups, greet_one, 0)
    pl.semaphore_wait(barrier, groups - 1)

    def exchange(source, target, send_sems, recv_sems):
        def start(i, carry):
            peer = lax.rem(me + i, groups)
            pltpu.make_async_remote_copy(
                src_ref=source.at[peer],
                dst_ref=target.at[me],
                send_sem=send_sems.at[i],
                recv_sem=recv_sems.at[i],
                device_id={"tp": peer},
                device_id_type=pl.DeviceIdType.MESH,
            ).start()
            return carry

        lax.fori_loop(1, groups, start, 0)
        target[me] = source[me]

        def finish(i, carry):
            peer = lax.rem(me + i, groups)
            origin = lax.rem(me + groups - i, groups)
            pltpu.make_async_remote_copy(
                src_ref=source.at[peer],
                dst_ref=target.at[origin],
                send_sem=send_sems.at[i],
                recv_sem=recv_sems.at[i],
                device_id={"tp": peer},
                device_id_type=pl.DeviceIdType.MESH,
            ).wait()
            return carry

        lax.fori_loop(1, groups, finish, 0)

    exchange(sent_ref, got_ref, send0, recv0)
    attend_kernel(len_ref, got_ref, cache_ref, att_ref, pairs_ref)
    exchange(att_ref, back_ref, send1, recv1)


def attend_slots(lengths, outgoing, cached):
    groups, slot_rows, lanes = outgoing.shape
    slots, cached_len, width = cached.shape
    vmem = pl.BlockSpec(memory_space=pltpu.VMEM)
    return pl.pallas_call(
        exchange_kernel,
        out_shape=(
            jax.ShapeDtypeStruct((groups, slot_rows, HD), jnp.bfloat16),
            jax.ShapeDtypeStruct((slot_rows, width), jnp.bfloat16),
        ),
        in_specs=[pl.BlockSpec(memory_space=pltpu.SMEM), vmem, vmem],
        out_specs=(vmem, vmem),
        scratch_shapes=[
            pltpu.VMEM((groups, slot_rows, lanes), jnp.bfloat16),
            pltpu.VMEM((groups, slot_rows, HD), jnp.bfloat16),
            pltpu.SemaphoreType.DMA((groups,)),
            pltpu.SemaphoreType.DMA((groups,)),
            pltpu.SemaphoreType.DMA((groups,)),
            pltpu.SemaphoreType.DMA((groups,)),
        ],
        compiler_params=pltpu.CompilerParams(collective_id=2, has_side_effects=True),
    )(lengths, outgoing, cached.reshape(slots * cached_len, width))


def reduce_kernel(
    slot_ref, heads_ref, hid_ref, wo_hbm, out_ref,
    p_ref, wo_ref, res_ref, got0, got1, stage0, stage1,
    load_sem, shift_send, shift_recv, send_sems, recv_sems,
):
    me = lax.axis_index("tp")
    section = lax.axis_index("section")
    sections = lax.axis_size("section")
    after = lax.rem(section + 1, sections)
    before = lax.rem(section + sections - 1, sections)
    mx = me // NY
    my = lax.rem(me, NY)
    near = neighbours(mx, my)
    width = hid_ref.shape[1]
    parts = splits(width)
    got = (got0, got1)
    stage = (stage0, stage1)
    load = pltpu.make_async_copy(wo_hbm, wo_ref, load_sem)
    load.start()
    barrier = pltpu.get_barrier_semaphore()
    for device in near.values():
        pl.semaphore_signal(
            barrier, inc=1, device_id={"tp": device}, device_id_type=pl.DeviceIdType.MESH
        )
    pl.semaphore_signal(
        barrier, inc=1, device_id={"section": before}, device_id_type=pl.DeviceIdType.MESH
    )
    groups, count = p_ref.shape[:2]
    tokens = groups * count
    slot_rows = heads_ref.shape[0] * heads_ref.shape[1]
    chosen = slot_matrix(slot_ref, slot_rows)
    heads = lax.dot_general(
        chosen, heads_ref[...].reshape(slot_rows, heads_ref.shape[2]),
        (((0,), (0,)), ((), ())), preferred_element_type=jnp.float32,
    ).astype(jnp.bfloat16)
    load.wait()
    step = 256

    def multiply(mode):
        start, size = parts[mode]

        def one(k, carry):
            cols = pl.ds(pl.multiple_of(start + k * step, LANES), step)
            piece = jnp.dot(heads, wo_ref[:, cols], preferred_element_type=jnp.float32)
            p_ref[:, :, cols] = piece.reshape(groups, count, step).astype(jnp.bfloat16)
            return carry

        lax.fori_loop(0, size // step, one, 0)

    started = []

    def total(mode, dx, dy):
        start, size = parts[mode]
        block = block_at(mx, my, dx, dy)
        summed = p_ref[block, :, pl.ds(start, size)].astype(jnp.float32)
        for link in children(mode, dx, dy):
            slot = place_of(*moved(*link, dx, dy))
            pltpu.make_async_remote_copy(
                src_ref=stage[mode].at[slot],
                dst_ref=got[mode].at[slot],
                send_sem=send_sems.at[mode, slot],
                recv_sem=recv_sems.at[mode, slot],
                device_id={"tp": near[link]},
                device_id_type=pl.DeviceIdType.MESH,
            ).wait_recv()
            summed = summed + got[mode][slot].astype(jnp.float32)
        return summed

    def send(mode, dx, dy, source):
        slot = place_of(dx, dy)
        axis, sign = parent(mode, dx, dy)
        sent = pltpu.make_async_remote_copy(
            src_ref=source,
            dst_ref=got[mode].at[slot],
            send_sem=send_sems.at[mode, slot],
            recv_sem=recv_sems.at[mode, slot],
            device_id={"tp": near[axis, -sign]},
            device_id_type=pl.DeviceIdType.MESH,
        )
        sent.start()
        started.append(sent)

    def send_leaf(mode, dx, dy):
        start, size = parts[mode]
        send(mode, dx, dy, p_ref.at[block_at(mx, my, dx, dy), :, pl.ds(start, size)])

    def shift(mode):
        start, size = parts[mode]
        cols = pl.ds(start, size)
        return pltpu.make_async_remote_copy(
            src_ref=res_ref.at[:, cols],
            dst_ref=out_ref.at[:, cols],
            send_sem=shift_send.at[mode],
            recv_sem=shift_recv.at[mode],
            device_id={"section": after},
            device_id_type=pl.DeviceIdType.MESH,
        )

    order = arrival_order([part[1] * 16 / 46e3 for part in parts])[::-1]
    multiply(1)
    pl.semaphore_wait(barrier, len(near) + 1)
    early = [event for event in order[:16] if event[0] == 1 and not children(*event)]
    for event in early:
        send_leaf(*event)
    multiply(0)
    for event in order:
        if event in early:
            continue
        mode, dx, dy = event
        start, size = parts[mode]
        if (dx, dy) == (0, 0):
            cols = pl.ds(start, size)
            summed = total(mode, dx, dy) + hid_ref[:, cols].astype(jnp.float32)
            res_ref[:, cols] = summed.astype(jnp.bfloat16)
            shift(mode).start()
        elif children(mode, dx, dy):
            slot = place_of(dx, dy)
            stage[mode][slot] = total(mode, dx, dy).astype(jnp.bfloat16)
            send(mode, dx, dy, stage[mode].at[slot])
        else:
            send_leaf(mode, dx, dy)
    for sent in started:
        sent.wait_send()
    for mode in (0, 1):
        shift(mode).wait()


def reduce_rows(slot_tokens, heads, residual, weight_out):
    count, width = residual.shape
    groups = NX * NY
    parts = splits(width)
    vmem = pl.BlockSpec(memory_space=pltpu.VMEM)
    return pl.pallas_call(
        reduce_kernel,
        out_shape=jax.ShapeDtypeStruct((count, width), jnp.bfloat16),
        in_specs=[vmem, vmem, vmem, pl.BlockSpec(memory_space=pl.ANY)],
        out_specs=vmem,
        scratch_shapes=[
            pltpu.VMEM((groups, count, width), jnp.bfloat16),
            pltpu.VMEM(weight_out.shape, jnp.bfloat16),
            pltpu.VMEM((count, width), jnp.bfloat16),
            pltpu.VMEM((groups, count, parts[0][1]), jnp.bfloat16),
            pltpu.VMEM((groups, count, parts[1][1]), jnp.bfloat16),
            pltpu.VMEM((groups, count, parts[0][1]), jnp.bfloat16),
            pltpu.VMEM((groups, count, parts[1][1]), jnp.bfloat16),
            pltpu.SemaphoreType.DMA,
            pltpu.SemaphoreType.DMA((2,)),
            pltpu.SemaphoreType.DMA((2,)),
            pltpu.SemaphoreType.DMA((2, groups)),
            pltpu.SemaphoreType.DMA((2, groups)),
        ],
        compiler_params=pltpu.CompilerParams(collective_id=1, has_side_effects=True),
    )(slot_tokens, heads, residual, weight_out)


def owner_ranks(owners):
    count_all = owners.shape[0]
    same_owner = owners[:, None] == owners[None, :]
    position = jnp.arange(count_all, dtype=jnp.int32)
    earlier = position[None, :] < position[:, None]
    return jnp.sum(jnp.where(same_owner & earlier, 1, 0), axis=1).astype(jnp.int32)


def on_device(
    hidden, norm_gain, w_query, w_keyval, w_out, kv_cache, owner_map, accepted, context, draft_ids
):
    my_index = lax.axis_index("tp")
    owners = owner_map[0]
    accepts = accepted[0]
    lengths = context[0]
    token_ids = draft_ids[0]
    draft_steps = token_ids.shape[1]
    capacity = kv_cache.shape[1]
    slot_rows = capacity * draft_steps
    slot_of = owners * capacity + owner_ranks(owners)
    step_ids = jnp.arange(draft_steps, dtype=jnp.int32)
    slot_tokens = (slot_of[:, None] * draft_steps + step_ids[None, :]).reshape(1, -1)
    my_slots = my_index * capacity + jnp.arange(capacity, dtype=jnp.int32)
    mine = my_slots[:, None] == slot_of[None, :]
    my_lengths = jnp.sum(jnp.where(mine, lengths[None, :], 0), axis=1)
    my_accepts = jnp.sum(jnp.where(mine, accepts[None, :], 0), axis=1)
    my_ids = jnp.sum(jnp.where(mine[:, :, None], token_ids[None, :, :], 0), axis=1)
    outgoing = project_rows(
        hidden[0], norm_gain, slot_tokens, w_query[0], w_keyval[0], slot_rows
    )
    returned, new_pairs = attend_slots(my_lengths, outgoing, kv_cache[0])
    shifted = reduce_rows(slot_tokens, returned, hidden[0], w_out[0])
    keep = step_ids[None, :] < my_accepts[:, None]
    kept_ids = jnp.where(keep, my_ids, -1).reshape(-1)
    committed = jnp.where(keep.reshape(-1)[:, None], new_pairs, jnp.zeros_like(new_pairs))
    return (shifted[None], committed[None], kept_ids[None])


def solution(mesh):
    placed = (
        P("section", "tp", None),
        P("section", None),
        P("section", None, "tp"),
        P("section", "tp", None),
        P("section", "tp", None),
        P("section", "tp", None, None),
        P("section", None),
        P("section", None),
        P("section", None),
        P("section", None, None),
    )
    return jax.shard_map(
        on_device,
        mesh=mesh,
        in_specs=placed,
        out_specs=(P("section", "tp", None), P("section", "tp", None), P("section", "tp")),
        check_vma=False,
    )
```

```python
import jax
import jax.numpy as jnp
from jax import lax
from jax.experimental import pallas as pl
from jax.experimental.pallas import tpu as pltpu
from jax.sharding import PartitionSpec as P

HEADS = 32
KVH = 4
HD = 128


epsilon = 1e-06


NX = 4
NY = 8
LANES = 128
XY_SHARE = 26 / 64


def splits(width):
    first = max(1, round(width // LANES * XY_SHARE)) * LANES
    return ((0, first), (first, width - first))


def far_positive(mode, axis, dx, dy):
    if mode == 0:
        return True if axis == 0 else dx % 2 == 0
    return dy % 2 == 0 if axis == 0 else False


def reach(mode, axis, sign, dx, dy):
    half = (NX if axis == 0 else NY) // 2
    return half if far_positive(mode, axis, dx, dy) == (sign > 0) else half - 1


def travelled(mode, axis, dx, dy):
    size = NX if axis == 0 else NY
    ahead = (-dx if axis == 0 else -dy) % size
    if ahead == 0:
        return 0
    if ahead <= reach(mode, axis, 1, dx, dy):
        return ahead
    return ahead - size


def children(mode, dx, dy):
    first, second = (0, 1) if mode == 0 else (1, 0)
    hops = []
    step1 = travelled(mode, first, dx, dy)
    step2 = travelled(mode, second, dx, dy)
    if step2 == 0:
        for sign in (1, -1):
            if step1 * sign >= 0 and abs(step1) < reach(mode, first, sign, dx, dy):
                hops.append((first, sign))
    for sign in (1, -1):
        if step2 * sign >= 0 and abs(step2) < reach(mode, second, sign, dx, dy):
            hops.append((second, sign))
    return hops


def moved(axis, sign, dx, dy):
    return ((dx - sign) % NX, dy) if axis == 0 else (dx, (dy - sign) % NY)


def parent(mode, dx, dy):
    first, second = (0, 1) if mode == 0 else (1, 0)
    step2 = travelled(mode, second, dx, dy)
    axis = second if step2 else first
    return (axis, 1 if travelled(mode, axis, dx, dy) > 0 else -1)


def arrival_order(weights):
    free = {}
    order = []
    pending = [(0.0, 0, 0, 0), (0.0, 1, 0, 0)]
    while pending:
        pending.sort()
        now, mode, dx, dy = pending.pop(0)
        order.append((mode, dx, dy))
        for axis, sign in children(mode, dx, dy):
            begin = max(now, free.get((axis, sign), 0.0))
            free[axis, sign] = begin + weights[mode]
            pending.append((begin + weights[mode] + 1.6, mode) + moved(axis, sign, dx, dy))
    return order


def place_of(dx, dy):
    return dx * NY + dy


def neighbours(mx, my):
    return {
        (0, 1): lax.rem(mx + 1, NX) * NY + my,
        (0, -1): lax.rem(mx + NX - 1, NX) * NY + my,
        (1, 1): mx * NY + lax.rem(my + 1, NY),
        (1, -1): mx * NY + lax.rem(my + NY - 1, NY),
    }


def greet(devices):
    barrier = pltpu.get_barrier_semaphore()
    for device in devices:
        pl.semaphore_signal(
            barrier, inc=1, device_id={"tp": device}, device_id_type=pl.DeviceIdType.MESH
        )
    pl.semaphore_wait(barrier, len(devices))


def block_at(mx, my, dx, dy):
    return lax.rem(mx + dx, NX) * NY + lax.rem(my + dy, NY)


def as_column(row):
    size = row.shape[1]
    first = lax.broadcasted_iota(jnp.int32, (size, size), 0)
    second = lax.broadcasted_iota(jnp.int32, (size, size), 1)
    return jnp.sum(jnp.where(first == second, row, 0), axis=1, keepdims=True)


def slot_column(owners, capacity):
    size = owners.shape[1]
    column = as_column(owners)
    request = lax.broadcasted_iota(jnp.int32, (size, size), 0)
    other = lax.broadcasted_iota(jnp.int32, (size, size), 1)
    earlier = (column == owners) & (other < request)
    return column * capacity + jnp.sum(jnp.where(earlier, 1, 0), axis=1, keepdims=True)


def as_row(column):
    size = column.shape[0]
    first = lax.broadcasted_iota(jnp.int32, (size, size), 0)
    second = lax.broadcasted_iota(jnp.int32, (size, size), 1)
    return jnp.sum(jnp.where(first == second, column, 0), axis=0, keepdims=True)


def slot_matrix(owner_ref, tokens, rows):
    owners = owner_ref[...]
    requests = owners.shape[1]
    steps = tokens // requests
    capacity = rows // (NX * NY * steps)
    column = slot_column(owners, capacity)
    request = lax.broadcasted_iota(jnp.int32, (requests, tokens), 0)
    token = lax.broadcasted_iota(jnp.int32, (requests, tokens), 1)
    slots = jnp.sum(jnp.where(request == token // steps, column, 0), axis=0, keepdims=True)
    step = lax.broadcasted_iota(jnp.int32, (1, tokens), 1) % steps
    row = lax.broadcasted_iota(jnp.int32, (rows, tokens), 0)
    return jnp.where(row == slots * steps + step, 1.0, 0.0).astype(jnp.bfloat16)


def project_kernel(
    hid_ref, gain_ref, owner_ref, wq_hbm, wp_hbm, out_ref,
    x_ref, all_ref, wq_ref, wp_ref, acc_ref, chosen_ref, load_sems, send_sems, recv_sems,
):
    me = lax.axis_index("tp")
    mx = me // NY
    my = lax.rem(me, NY)
    near = neighbours(mx, my)
    width = hid_ref.shape[1]
    parts = splits(width)
    loads = [
        pltpu.make_async_copy(wq_hbm, wq_ref, load_sems.at[0]),
        pltpu.make_async_copy(wp_hbm, wp_ref, load_sems.at[1]),
    ]
    for load in loads:
        load.start()
    rows = hid_ref[...].astype(jnp.float32)
    inverse_rms = lax.rsqrt(jnp.mean(rows * rows, axis=1, keepdims=True) + epsilon)
    x_ref[...] = (rows * inverse_rms * gain_ref[...]).astype(jnp.bfloat16)
    greet(list(near.values()))

    def copy(mode, dx, dy, link):
        start, size = parts[mode]
        there = place_of(*moved(*link, dx, dy))
        cols = pl.ds(start, size)
        block = block_at(mx, my, dx, dy)
        source = x_ref.at[:, cols] if (dx, dy) == (0, 0) else all_ref.at[block, :, cols]
        return pltpu.make_async_remote_copy(
            src_ref=source,
            dst_ref=all_ref.at[block, :, cols],
            send_sem=send_sems.at[mode, there],
            recv_sem=recv_sems.at[mode, there],
            device_id={"tp": near[link]},
            device_id_type=pl.DeviceIdType.MESH,
        )

    started = []
    order = arrival_order([part[1] * 16 / 46e3 for part in parts])
    for mode, dx, dy in order:
        if (dx, dy) != (0, 0):
            start, size = parts[mode]
            landed = all_ref.at[block_at(mx, my, dx, dy), :, pl.ds(start, size)]
            pltpu.make_async_remote_copy(
                src_ref=landed,
                dst_ref=landed,
                send_sem=send_sems.at[mode, place_of(dx, dy)],
                recv_sem=recv_sems.at[mode, place_of(dx, dy)],
                device_id={"tp": near[parent(mode, dx, dy)]},
                device_id_type=pl.DeviceIdType.MESH,
            ).wait_recv()
        for link in children(mode, dx, dy):
            sent = copy(mode, dx, dy, link)
            sent.start()
            started.append(sent)
        if len(started) == 8:
            all_ref[me] = x_ref[...]
            chosen_ref[...] = slot_matrix(owner_ref, chosen_ref.shape[1], chosen_ref.shape[0])
            for load in loads:
                load.wait()
    groups, count = all_ref.shape[:2]
    tokens = groups * count
    query_cols = wq_ref.shape[1]
    pair_cols = wp_ref.shape[0]
    step = width // 8
    acc_ref[...] = jnp.zeros_like(acc_ref)

    def add(k, carry):
        cols = pl.ds(pl.multiple_of(k * step, step), step)
        x = all_ref[:, :, cols].reshape(tokens, step)
        acc_ref[:, :query_cols] += jnp.dot(
            x, wq_ref[cols, :], preferred_element_type=jnp.float32
        )
        acc_ref[:, query_cols:] += lax.dot_general(
            x, wp_ref[:, cols], (((1,), (1,)), ((), ())), preferred_element_type=jnp.float32
        )
        return carry

    lax.fori_loop(0, 8, add, 0)
    queries = acc_ref[:, :query_cols].astype(jnp.bfloat16)
    pairs = acc_ref[:, query_cols:].astype(jnp.bfloat16)
    lane = lax.broadcasted_iota(jnp.int32, (pair_cols, LANES), 1)
    source = lax.broadcasted_iota(jnp.int32, (pair_cols, LANES), 0)
    offset = lax.rem(me, LANES // pair_cols) * pair_cols
    spread = jnp.where(lane == source + offset, 1.0, 0.0).astype(jnp.bfloat16)
    placed = jnp.dot(pairs, spread, preferred_element_type=jnp.float32).astype(jnp.bfloat16)
    chosen = chosen_ref[...]
    out_shape = out_ref.shape[:2] + (LANES,)
    out_ref[:, :, :LANES] = (
        jnp.dot(chosen, queries, preferred_element_type=jnp.float32)
        .reshape(out_shape).astype(jnp.bfloat16)
    )
    out_ref[:, :, LANES:] = (
        jnp.dot(chosen, placed, preferred_element_type=jnp.float32)
        .reshape(out_shape).astype(jnp.bfloat16)
    )
    for sent in started:
        sent.wait_send()


def project_rows(hidden, gain, owners, weight_query, weight_pair, slot_rows):
    count, width = hidden.shape
    groups = NX * NY
    vmem = pl.BlockSpec(memory_space=pltpu.VMEM)
    hbm = pl.BlockSpec(memory_space=pl.ANY)
    query_cols = weight_query.shape[1]
    pair_cols = weight_pair.shape[0]
    return pl.pallas_call(
        project_kernel,
        out_shape=jax.ShapeDtypeStruct((groups, slot_rows, 2 * LANES), jnp.bfloat16),
        in_specs=[vmem, vmem, vmem, hbm, hbm],
        out_specs=vmem,
        scratch_shapes=[
            pltpu.VMEM((count, width), jnp.bfloat16),
            pltpu.VMEM((groups, count, width), jnp.bfloat16),
            pltpu.VMEM(weight_query.shape, jnp.bfloat16),
            pltpu.VMEM(weight_pair.shape, jnp.bfloat16),
            pltpu.VMEM((groups * count, query_cols + pair_cols), jnp.float32),
            pltpu.VMEM((groups * slot_rows, groups * count), jnp.bfloat16),
            pltpu.SemaphoreType.DMA((2,)),
            pltpu.SemaphoreType.DMA((2, groups)),
            pltpu.SemaphoreType.DMA((2, groups)),
        ],
        compiler_params=pltpu.CompilerParams(collective_id=0, has_side_effects=True),
    )(hidden, gain, owners, weight_query, weight_pair)


def attend_kernel(allowed, keep, got_ref, cache_ref, out_ref, pairs_ref):
    slot_rows = got_ref.shape[1]
    per_kv = HEADS // KVH
    rows = per_kv * slot_rows
    pieces = got_ref.shape[0] // (2 * KVH)
    for e in range(KVH):
        cols = slice(e * HD, (e + 1) * HD)
        value_cols = slice((KVH + e) * HD, (KVH + e + 1) * HD)

        def joined(first):
            total = got_ref[first, :, LANES:].astype(jnp.float32)
            for i in range(1, pieces):
                total = total + got_ref[first + i, :, LANES:].astype(jnp.float32)
            return total.astype(jnp.bfloat16)

        new_keys = joined(e * pieces)
        new_values = joined((KVH + e) * pieces)
        pairs_ref[:, cols] = jnp.where(keep, new_keys, jnp.zeros_like(new_keys))
        pairs_ref[:, value_cols] = jnp.where(keep, new_values, jnp.zeros_like(new_values))
        keys = jnp.concatenate([cache_ref[:, cols], new_keys], axis=0)
        values = jnp.concatenate([cache_ref[:, value_cols], new_values], axis=0)
        queries = got_ref[e * per_kv : (e + 1) * per_kv, :, :LANES].reshape(rows, HD)
        scores = lax.dot_general(
            queries, keys, (((1,), (1,)), ((), ())), preferred_element_type=jnp.float32
        ) * HD ** (-0.5)
        scores = jnp.where(allowed, scores, -jnp.inf)
        weights = jnp.exp(scores - jnp.max(scores, axis=1, keepdims=True))
        probs = (weights / jnp.sum(weights, axis=1, keepdims=True)).astype(jnp.bfloat16)
        attended = jnp.dot(probs, values, preferred_element_type=jnp.float32)
        out_ref[e * per_kv : (e + 1) * per_kv] = attended.reshape(
            per_kv, slot_rows, HD
        ).astype(jnp.bfloat16)


def exchange_kernel(
    owner_ref, length_ref, accept_ref, id_ref, sent_ref, cache_ref,
    back_ref, pairs_ref, kept_ref, got_ref, att_ref, send0, recv0, send1, recv1,
):
    me = lax.axis_index("tp")
    groups = sent_ref.shape[0]
    barrier = pltpu.get_barrier_semaphore()

    def greet_one(i, carry):
        pl.semaphore_signal(
            barrier, inc=1, device_id={"tp": lax.rem(me + i, groups)},
            device_id_type=pl.DeviceIdType.MESH,
        )
        return carry

    lax.fori_loop(1, groups, greet_one, 0)
    slot_rows = sent_ref.shape[1]
    requests = owner_ref.shape[1]
    steps = id_ref.shape[0]
    slots = slot_rows // steps
    cached_rows = cache_ref.shape[0]
    cached_len = cached_rows // slots
    slot_row = as_row(slot_column(owner_ref[...], slots))
    row = lax.broadcasted_iota(jnp.int32, (slot_rows, requests), 0)
    mine = me * slots + row // steps == slot_row
    ids = jnp.zeros((slot_rows, requests), jnp.int32)
    for j in range(steps):
        ids = jnp.where(row % steps == j, id_ref[j : j + 1, :], ids)

    def held(values):
        return jnp.sum(jnp.where(mine, values, 0), axis=1, keepdims=True)

    lengths = held(length_ref[...])
    step = lax.broadcasted_iota(jnp.int32, (slot_rows, 1), 0) % steps
    keep = step < held(accept_ref[...])
    kept_ref[...] = as_row(jnp.where(keep, held(ids), -1))
    span = cached_rows + slot_rows
    row = lax.broadcasted_iota(jnp.int32, (slot_rows, span), 0)
    col = lax.broadcasted_iota(jnp.int32, (slot_rows, span), 1)
    fresh = col - cached_rows
    in_cache = (fresh < 0) & (col // cached_len == row // steps) & (col % cached_len < lengths)
    in_draft = (fresh >= 0) & (fresh // steps == row // steps) & (fresh <= row)
    flags = jnp.where(in_cache | in_draft, 1, 0)
    allowed = jnp.concatenate([flags] * (HEADS // KVH), axis=0) == 1
    pl.semaphore_wait(barrier, groups - 1)

    def exchange(source, target, send_sems, recv_sems):
        def start(i, carry):
            peer = lax.rem(me + i, groups)
            pltpu.make_async_remote_copy(
                src_ref=source.at[peer],
                dst_ref=target.at[me],
                send_sem=send_sems.at[i],
                recv_sem=recv_sems.at[i],
                device_id={"tp": peer},
                device_id_type=pl.DeviceIdType.MESH,
            ).start()
            return carry

        lax.fori_loop(1, groups, start, 0)
        target[me] = source[me]

        def finish(i, carry):
            peer = lax.rem(me + i, groups)
            origin = lax.rem(me + groups - i, groups)
            pltpu.make_async_remote_copy(
                src_ref=source.at[peer],
                dst_ref=target.at[origin],
                send_sem=send_sems.at[i],
                recv_sem=recv_sems.at[i],
                device_id={"tp": peer},
                device_id_type=pl.DeviceIdType.MESH,
            ).wait()
            return carry

        lax.fori_loop(1, groups, finish, 0)

    exchange(sent_ref, got_ref, send0, recv0)
    attend_kernel(allowed, keep, got_ref, cache_ref, att_ref, pairs_ref)
    exchange(att_ref, back_ref, send1, recv1)


def attend_slots(owners, lengths, accepts, ids, outgoing, cached):
    groups, slot_rows, lanes = outgoing.shape
    slots, cached_len, width = cached.shape
    vmem = pl.BlockSpec(memory_space=pltpu.VMEM)
    return pl.pallas_call(
        exchange_kernel,
        out_shape=(
            jax.ShapeDtypeStruct((groups, slot_rows, HD), jnp.bfloat16),
            jax.ShapeDtypeStruct((slot_rows, width), jnp.bfloat16),
            jax.ShapeDtypeStruct((1, slot_rows), jnp.int32),
        ),
        in_specs=[vmem] * 6,
        out_specs=(vmem, vmem, vmem),
        scratch_shapes=[
            pltpu.VMEM((groups, slot_rows, lanes), jnp.bfloat16),
            pltpu.VMEM((groups, slot_rows, HD), jnp.bfloat16),
            pltpu.SemaphoreType.DMA((groups,)),
            pltpu.SemaphoreType.DMA((groups,)),
            pltpu.SemaphoreType.DMA((groups,)),
            pltpu.SemaphoreType.DMA((groups,)),
        ],
        compiler_params=pltpu.CompilerParams(collective_id=2, has_side_effects=True),
    )(owners, lengths, accepts, ids, outgoing, cached.reshape(slots * cached_len, width))


def reduce_kernel(
    owner_ref, heads_ref, hid_ref, wo_hbm, out_ref,
    p_ref, wo_ref, res_ref, got0, got1, stage0, stage1,
    load_sem, shift_send, shift_recv, send_sems, recv_sems,
):
    me = lax.axis_index("tp")
    section = lax.axis_index("section")
    sections = lax.axis_size("section")
    after = lax.rem(section + 1, sections)
    before = lax.rem(section + sections - 1, sections)
    mx = me // NY
    my = lax.rem(me, NY)
    near = neighbours(mx, my)
    width = hid_ref.shape[1]
    parts = splits(width)
    got = (got0, got1)
    stage = (stage0, stage1)
    load = pltpu.make_async_copy(wo_hbm, wo_ref, load_sem)
    load.start()
    barrier = pltpu.get_barrier_semaphore()
    for device in near.values():
        pl.semaphore_signal(
            barrier, inc=1, device_id={"tp": device}, device_id_type=pl.DeviceIdType.MESH
        )
    pl.semaphore_signal(
        barrier, inc=1, device_id={"section": before}, device_id_type=pl.DeviceIdType.MESH
    )
    groups, count = p_ref.shape[:2]
    tokens = groups * count
    slot_rows = heads_ref.shape[0] * heads_ref.shape[1]
    chosen = slot_matrix(owner_ref, tokens, slot_rows)
    heads = lax.dot_general(
        chosen, heads_ref[...].reshape(slot_rows, heads_ref.shape[2]),
        (((0,), (0,)), ((), ())), preferred_element_type=jnp.float32,
    ).astype(jnp.bfloat16)
    load.wait()
    step = 256

    def multiply(mode):
        start, size = parts[mode]

        def one(k, carry):
            cols = pl.ds(pl.multiple_of(start + k * step, LANES), step)
            piece = jnp.dot(heads, wo_ref[:, cols], preferred_element_type=jnp.float32)
            p_ref[:, :, cols] = piece.reshape(groups, count, step).astype(jnp.bfloat16)
            return carry

        lax.fori_loop(0, size // step, one, 0)

    started = []

    def total(mode, dx, dy):
        start, size = parts[mode]
        block = block_at(mx, my, dx, dy)
        summed = p_ref[block, :, pl.ds(start, size)].astype(jnp.float32)
        for link in children(mode, dx, dy):
            slot = place_of(*moved(*link, dx, dy))
            pltpu.make_async_remote_copy(
                src_ref=stage[mode].at[slot],
                dst_ref=got[mode].at[slot],
                send_sem=send_sems.at[mode, slot],
                recv_sem=recv_sems.at[mode, slot],
                device_id={"tp": near[link]},
                device_id_type=pl.DeviceIdType.MESH,
            ).wait_recv()
            summed = summed + got[mode][slot].astype(jnp.float32)
        return summed

    def send(mode, dx, dy, source):
        slot = place_of(dx, dy)
        axis, sign = parent(mode, dx, dy)
        sent = pltpu.make_async_remote_copy(
            src_ref=source,
            dst_ref=got[mode].at[slot],
            send_sem=send_sems.at[mode, slot],
            recv_sem=recv_sems.at[mode, slot],
            device_id={"tp": near[axis, -sign]},
            device_id_type=pl.DeviceIdType.MESH,
        )
        sent.start()
        started.append(sent)

    def send_leaf(mode, dx, dy):
        start, size = parts[mode]
        send(mode, dx, dy, p_ref.at[block_at(mx, my, dx, dy), :, pl.ds(start, size)])

    def shift(mode):
        start, size = parts[mode]
        cols = pl.ds(start, size)
        return pltpu.make_async_remote_copy(
            src_ref=res_ref.at[:, cols],
            dst_ref=out_ref.at[:, cols],
            send_sem=shift_send.at[mode],
            recv_sem=shift_recv.at[mode],
            device_id={"section": after},
            device_id_type=pl.DeviceIdType.MESH,
        )

    order = arrival_order([part[1] * 16 / 46e3 for part in parts])[::-1]
    multiply(1)
    pl.semaphore_wait(barrier, len(near) + 1)
    early = [event for event in order[:16] if event[0] == 1 and not children(*event)]
    for event in early:
        send_leaf(*event)
    multiply(0)
    for event in order:
        if event in early:
            continue
        mode, dx, dy = event
        start, size = parts[mode]
        if (dx, dy) == (0, 0):
            cols = pl.ds(start, size)
            summed = total(mode, dx, dy) + hid_ref[:, cols].astype(jnp.float32)
            res_ref[:, cols] = summed.astype(jnp.bfloat16)
            shift(mode).start()
        elif children(mode, dx, dy):
            slot = place_of(dx, dy)
            stage[mode][slot] = total(mode, dx, dy).astype(jnp.bfloat16)
            send(mode, dx, dy, stage[mode].at[slot])
        else:
            send_leaf(mode, dx, dy)
    for sent in started:
        sent.wait_send()
    for mode in (0, 1):
        shift(mode).wait()


def reduce_rows(owners, heads, residual, weight_out):
    count, width = residual.shape
    groups = NX * NY
    parts = splits(width)
    vmem = pl.BlockSpec(memory_space=pltpu.VMEM)
    return pl.pallas_call(
        reduce_kernel,
        out_shape=jax.ShapeDtypeStruct((count, width), jnp.bfloat16),
        in_specs=[vmem, vmem, vmem, pl.BlockSpec(memory_space=pl.ANY)],
        out_specs=vmem,
        scratch_shapes=[
            pltpu.VMEM((groups, count, width), jnp.bfloat16),
            pltpu.VMEM(weight_out.shape, jnp.bfloat16),
            pltpu.VMEM((count, width), jnp.bfloat16),
            pltpu.VMEM((groups, count, parts[0][1]), jnp.bfloat16),
            pltpu.VMEM((groups, count, parts[1][1]), jnp.bfloat16),
            pltpu.VMEM((groups, count, parts[0][1]), jnp.bfloat16),
            pltpu.VMEM((groups, count, parts[1][1]), jnp.bfloat16),
            pltpu.SemaphoreType.DMA,
            pltpu.SemaphoreType.DMA((2,)),
            pltpu.SemaphoreType.DMA((2,)),
            pltpu.SemaphoreType.DMA((2, groups)),
            pltpu.SemaphoreType.DMA((2, groups)),
        ],
        compiler_params=pltpu.CompilerParams(collective_id=1, has_side_effects=True),
    )(owners, heads, residual, weight_out)


def on_device(
    hidden, norm_gain, w_query, w_keyval, w_out, kv_cache, owner_map, accepted, context, draft_ids
):
    slot_rows = kv_cache.shape[1] * draft_ids.shape[2]
    outgoing = project_rows(
        hidden[0], norm_gain, owner_map, w_query[0], w_keyval[0], slot_rows
    )
    returned, committed, kept_ids = attend_slots(
        owner_map, context, accepted, draft_ids[0].T, outgoing, kv_cache[0]
    )
    shifted = reduce_rows(owner_map, returned, hidden[0], w_out[0])
    return (shifted[None], committed[None], kept_ids)


def solution(mesh):
    placed = (
        P("section", "tp", None),
        P("section", None),
        P("section", None, "tp"),
        P("section", "tp", None),
        P("section", "tp", None),
        P("section", "tp", None, None),
        P("section", None),
        P("section", None),
        P("section", None),
        P("section", None, None),
    )
    return jax.shard_map(
        on_device,
        mesh=mesh,
        in_specs=placed,
        out_specs=(P("section", "tp", None), P("section", "tp", None), P("section", "tp")),
        check_vma=False,
    )
```

```python
import jax
import jax.numpy as jnp
from jax import lax
from jax.experimental import pallas as pl
from jax.experimental.pallas import tpu as pltpu
from jax.sharding import PartitionSpec as P

HEADS = 32
KVH = 4
HD = 128


epsilon = 1e-06


NX = 4
NY = 8
LANES = 128
XY_SHARE = 26 / 64


def splits(width):
    first = max(1, round(width // LANES * XY_SHARE)) * LANES
    return ((0, first), (first, width - first))


def far_positive(mode, axis, dx, dy):
    if mode == 0:
        return True if axis == 0 else dx % 2 == 0
    return dy % 2 == 0 if axis == 0 else False


def reach(mode, axis, sign, dx, dy):
    half = (NX if axis == 0 else NY) // 2
    return half if far_positive(mode, axis, dx, dy) == (sign > 0) else half - 1


def travelled(mode, axis, dx, dy):
    size = NX if axis == 0 else NY
    ahead = (-dx if axis == 0 else -dy) % size
    if ahead == 0:
        return 0
    if ahead <= reach(mode, axis, 1, dx, dy):
        return ahead
    return ahead - size


def children(mode, dx, dy):
    first, second = (0, 1) if mode == 0 else (1, 0)
    hops = []
    step1 = travelled(mode, first, dx, dy)
    step2 = travelled(mode, second, dx, dy)
    if step2 == 0:
        for sign in (1, -1):
            if step1 * sign >= 0 and abs(step1) < reach(mode, first, sign, dx, dy):
                hops.append((first, sign))
    for sign in (1, -1):
        if step2 * sign >= 0 and abs(step2) < reach(mode, second, sign, dx, dy):
            hops.append((second, sign))
    return hops


def moved(axis, sign, dx, dy):
    return ((dx - sign) % NX, dy) if axis == 0 else (dx, (dy - sign) % NY)


def parent(mode, dx, dy):
    first, second = (0, 1) if mode == 0 else (1, 0)
    step2 = travelled(mode, second, dx, dy)
    axis = second if step2 else first
    return (axis, 1 if travelled(mode, axis, dx, dy) > 0 else -1)


def arrival_order(weights):
    free = {}
    order = []
    pending = [(0.0, 0, 0, 0), (0.0, 1, 0, 0)]
    while pending:
        pending.sort()
        now, mode, dx, dy = pending.pop(0)
        order.append((mode, dx, dy))
        for axis, sign in children(mode, dx, dy):
            begin = max(now, free.get((axis, sign), 0.0))
            free[axis, sign] = begin + weights[mode]
            pending.append((begin + weights[mode] + 1.6, mode) + moved(axis, sign, dx, dy))
    return order


def place_of(dx, dy):
    return dx * NY + dy


def neighbours(mx, my):
    return {
        (0, 1): lax.rem(mx + 1, NX) * NY + my,
        (0, -1): lax.rem(mx + NX - 1, NX) * NY + my,
        (1, 1): mx * NY + lax.rem(my + 1, NY),
        (1, -1): mx * NY + lax.rem(my + NY - 1, NY),
    }


def greet(devices):
    barrier = pltpu.get_barrier_semaphore()
    for device in devices:
        pl.semaphore_signal(
            barrier, inc=1, device_id={"tp": device}, device_id_type=pl.DeviceIdType.MESH
        )
    pl.semaphore_wait(barrier, len(devices))


def block_at(mx, my, dx, dy):
    return lax.rem(mx + dx, NX) * NY + lax.rem(my + dy, NY)


def as_column(row):
    size = row.shape[1]
    first = lax.broadcasted_iota(jnp.int32, (size, size), 0)
    second = lax.broadcasted_iota(jnp.int32, (size, size), 1)
    return jnp.sum(jnp.where(first == second, row, 0), axis=1, keepdims=True)


def slot_column(owners, capacity):
    size = owners.shape[1]
    column = as_column(owners)
    request = lax.broadcasted_iota(jnp.int32, (size, size), 0)
    other = lax.broadcasted_iota(jnp.int32, (size, size), 1)
    earlier = (column == owners) & (other < request)
    return column * capacity + jnp.sum(jnp.where(earlier, 1, 0), axis=1, keepdims=True)


def as_row(column):
    size = column.shape[0]
    first = lax.broadcasted_iota(jnp.int32, (size, size), 0)
    second = lax.broadcasted_iota(jnp.int32, (size, size), 1)
    return jnp.sum(jnp.where(first == second, column, 0), axis=0, keepdims=True)


def slot_matrix(owner_ref, tokens, rows):
    owners = owner_ref[...]
    requests = owners.shape[1]
    steps = tokens // requests
    capacity = rows // (NX * NY * steps)
    column = slot_column(owners, capacity)
    request = lax.broadcasted_iota(jnp.int32, (requests, tokens), 0)
    token = lax.broadcasted_iota(jnp.int32, (requests, tokens), 1)
    slots = jnp.sum(jnp.where(request == token // steps, column, 0), axis=0, keepdims=True)
    step = lax.broadcasted_iota(jnp.int32, (1, tokens), 1) % steps
    row = lax.broadcasted_iota(jnp.int32, (rows, tokens), 0)
    return jnp.where(row == slots * steps + step, 1.0, 0.0).astype(jnp.bfloat16)


def project_kernel(
    hid_ref, gain_ref, owner_ref, wq_hbm, wp_hbm, out_ref,
    x_ref, all_ref, wq_ref, wp_ref, turned_ref, acc_ref, chosen_ref, load_sems, send_sems, recv_sems,
):
    me = lax.axis_index("tp")
    mx = me // NY
    my = lax.rem(me, NY)
    near = neighbours(mx, my)
    width = hid_ref.shape[1]
    parts = splits(width)
    loads = [
        pltpu.make_async_copy(wq_hbm, wq_ref, load_sems.at[0]),
        pltpu.make_async_copy(wp_hbm, wp_ref, load_sems.at[1]),
    ]
    for load in loads:
        load.start()
    rows = hid_ref[...].astype(jnp.float32)
    inverse_rms = lax.rsqrt(jnp.mean(rows * rows, axis=1, keepdims=True) + epsilon)
    x_ref[...] = (rows * inverse_rms * gain_ref[...]).astype(jnp.bfloat16)
    greet(list(near.values()))

    def copy(mode, dx, dy, link):
        start, size = parts[mode]
        there = place_of(*moved(*link, dx, dy))
        cols = pl.ds(start, size)
        block = block_at(mx, my, dx, dy)
        source = x_ref.at[:, cols] if (dx, dy) == (0, 0) else all_ref.at[block, :, cols]
        return pltpu.make_async_remote_copy(
            src_ref=source,
            dst_ref=all_ref.at[block, :, cols],
            send_sem=send_sems.at[mode, there],
            recv_sem=recv_sems.at[mode, there],
            device_id={"tp": near[link]},
            device_id_type=pl.DeviceIdType.MESH,
        )

    started = []
    order = arrival_order([part[1] * 16 / 46e3 for part in parts])
    for mode, dx, dy in order:
        if (dx, dy) != (0, 0):
            start, size = parts[mode]
            landed = all_ref.at[block_at(mx, my, dx, dy), :, pl.ds(start, size)]
            pltpu.make_async_remote_copy(
                src_ref=landed,
                dst_ref=landed,
                send_sem=send_sems.at[mode, place_of(dx, dy)],
                recv_sem=recv_sems.at[mode, place_of(dx, dy)],
                device_id={"tp": near[parent(mode, dx, dy)]},
                device_id_type=pl.DeviceIdType.MESH,
            ).wait_recv()
        for link in children(mode, dx, dy):
            sent = copy(mode, dx, dy, link)
            sent.start()
            started.append(sent)
        if len(started) == 8:
            all_ref[me] = x_ref[...]
            chosen_ref[...] = slot_matrix(owner_ref, chosen_ref.shape[1], chosen_ref.shape[0])
            for load in loads:
                load.wait()
            turned_ref[...] = jnp.zeros_like(turned_ref)
            for k in range(8):
                cols = pl.ds(k * (width // 8), width // 8)
                turned_ref[cols, : wp_ref.shape[0]] = wp_ref[:, cols].T
    groups, count = all_ref.shape[:2]
    tokens = groups * count
    query_cols = wq_ref.shape[1]
    pair_cols = wp_ref.shape[0]
    step = width // 8
    acc_ref[...] = jnp.zeros_like(acc_ref)

    def add(k, carry):
        cols = pl.ds(pl.multiple_of(k * step, step), step)
        x = all_ref[:, :, cols].reshape(tokens, step)
        weights = jnp.concatenate([wq_ref[cols, :], turned_ref[cols, :]], axis=1)
        acc_ref[...] += jnp.dot(x, weights, preferred_element_type=jnp.float32)
        return carry

    lax.fori_loop(0, 8, add, 0)
    queries = acc_ref[:, :query_cols].astype(jnp.bfloat16)
    pairs = acc_ref[:, query_cols : query_cols + pair_cols].astype(jnp.bfloat16)
    lane = lax.broadcasted_iota(jnp.int32, (pair_cols, LANES), 1)
    source = lax.broadcasted_iota(jnp.int32, (pair_cols, LANES), 0)
    offset = lax.rem(me, LANES // pair_cols) * pair_cols
    spread = jnp.where(lane == source + offset, 1.0, 0.0).astype(jnp.bfloat16)
    placed = jnp.dot(pairs, spread, preferred_element_type=jnp.float32).astype(jnp.bfloat16)
    chosen = chosen_ref[...]
    out_shape = out_ref.shape[:2] + (LANES,)
    out_ref[:, :, :LANES] = (
        jnp.dot(chosen, queries, preferred_element_type=jnp.float32)
        .reshape(out_shape).astype(jnp.bfloat16)
    )
    out_ref[:, :, LANES:] = (
        jnp.dot(chosen, placed, preferred_element_type=jnp.float32)
        .reshape(out_shape).astype(jnp.bfloat16)
    )
    for sent in started:
        sent.wait_send()


def project_rows(hidden, gain, owners, weight_query, weight_pair, slot_rows):
    count, width = hidden.shape
    groups = NX * NY
    vmem = pl.BlockSpec(memory_space=pltpu.VMEM)
    hbm = pl.BlockSpec(memory_space=pl.ANY)
    query_cols = weight_query.shape[1]
    return pl.pallas_call(
        project_kernel,
        out_shape=jax.ShapeDtypeStruct((groups, slot_rows, 2 * LANES), jnp.bfloat16),
        in_specs=[vmem, vmem, vmem, hbm, hbm],
        out_specs=vmem,
        scratch_shapes=[
            pltpu.VMEM((count, width), jnp.bfloat16),
            pltpu.VMEM((groups, count, width), jnp.bfloat16),
            pltpu.VMEM(weight_query.shape, jnp.bfloat16),
            pltpu.VMEM(weight_pair.shape, jnp.bfloat16),
            pltpu.VMEM((width, LANES), jnp.bfloat16),
            pltpu.VMEM((groups * count, query_cols + LANES), jnp.float32),
            pltpu.VMEM((groups * slot_rows, groups * count), jnp.bfloat16),
            pltpu.SemaphoreType.DMA((2,)),
            pltpu.SemaphoreType.DMA((2, groups)),
            pltpu.SemaphoreType.DMA((2, groups)),
        ],
        compiler_params=pltpu.CompilerParams(collective_id=0, has_side_effects=True),
    )(hidden, gain, owners, weight_query, weight_pair)


def attend_kernel(allowed, keep, got_ref, cache_ref, out_ref, pairs_ref):
    slot_rows = got_ref.shape[1]
    per_kv = HEADS // KVH
    rows = per_kv * slot_rows
    pieces = got_ref.shape[0] // (2 * KVH)
    for e in range(KVH):
        cols = slice(e * HD, (e + 1) * HD)
        value_cols = slice((KVH + e) * HD, (KVH + e + 1) * HD)

        def joined(first):
            total = got_ref[first, :, LANES:].astype(jnp.float32)
            for i in range(1, pieces):
                total = total + got_ref[first + i, :, LANES:].astype(jnp.float32)
            return total.astype(jnp.bfloat16)

        new_keys = joined(e * pieces)
        new_values = joined((KVH + e) * pieces)
        pairs_ref[:, cols] = jnp.where(keep, new_keys, jnp.zeros_like(new_keys))
        pairs_ref[:, value_cols] = jnp.where(keep, new_values, jnp.zeros_like(new_values))
        keys = jnp.concatenate([cache_ref[:, cols], new_keys], axis=0)
        values = jnp.concatenate([cache_ref[:, value_cols], new_values], axis=0)
        queries = got_ref[e * per_kv : (e + 1) * per_kv, :, :LANES].reshape(rows, HD)
        scores = lax.dot_general(
            queries, keys, (((1,), (1,)), ((), ())), preferred_element_type=jnp.float32
        ) * HD ** (-0.5)
        scores = jnp.where(allowed, scores, -jnp.inf)
        weights = jnp.exp(scores - jnp.max(scores, axis=1, keepdims=True))
        probs = (weights / jnp.sum(weights, axis=1, keepdims=True)).astype(jnp.bfloat16)
        attended = jnp.dot(probs, values, preferred_element_type=jnp.float32)
        out_ref[e * per_kv : (e + 1) * per_kv] = attended.reshape(
            per_kv, slot_rows, HD
        ).astype(jnp.bfloat16)


def exchange_kernel(
    owner_ref, length_ref, accept_ref, id_ref, sent_ref, cache_ref,
    back_ref, pairs_ref, kept_ref, got_ref, att_ref, send0, recv0, send1, recv1,
):
    me = lax.axis_index("tp")
    groups = sent_ref.shape[0]
    barrier = pltpu.get_barrier_semaphore()

    def greet_one(i, carry):
        pl.semaphore_signal(
            barrier, inc=1, device_id={"tp": lax.rem(me + i, groups)},
            device_id_type=pl.DeviceIdType.MESH,
        )
        return carry

    lax.fori_loop(1, groups, greet_one, 0)
    slot_rows = sent_ref.shape[1]
    requests = owner_ref.shape[1]
    steps = id_ref.shape[0]
    slots = slot_rows // steps
    cached_rows = cache_ref.shape[0]
    cached_len = cached_rows // slots
    slot_row = as_row(slot_column(owner_ref[...], slots))
    row = lax.broadcasted_iota(jnp.int32, (slot_rows, requests), 0)
    mine = me * slots + row // steps == slot_row
    ids = jnp.zeros((slot_rows, requests), jnp.int32)
    for j in range(steps):
        ids = jnp.where(row % steps == j, id_ref[j : j + 1, :], ids)

    def held(values):
        return jnp.sum(jnp.where(mine, values, 0), axis=1, keepdims=True)

    lengths = held(length_ref[...])
    step = lax.broadcasted_iota(jnp.int32, (slot_rows, 1), 0) % steps
    keep = step < held(accept_ref[...])
    kept_ref[...] = as_row(jnp.where(keep, held(ids), -1))
    span = cached_rows + slot_rows
    row = lax.broadcasted_iota(jnp.int32, (slot_rows, span), 0)
    col = lax.broadcasted_iota(jnp.int32, (slot_rows, span), 1)
    fresh = col - cached_rows
    in_cache = (fresh < 0) & (col // cached_len == row // steps) & (col % cached_len < lengths)
    in_draft = (fresh >= 0) & (fresh // steps == row // steps) & (fresh <= row)
    flags = jnp.where(in_cache | in_draft, 1, 0)
    allowed = jnp.concatenate([flags] * (HEADS // KVH), axis=0) == 1
    pl.semaphore_wait(barrier, groups - 1)

    def exchange(source, target, send_sems, recv_sems):
        def start(i, carry):
            peer = lax.rem(me + i, groups)
            pltpu.make_async_remote_copy(
                src_ref=source.at[peer],
                dst_ref=target.at[me],
                send_sem=send_sems.at[i],
                recv_sem=recv_sems.at[i],
                device_id={"tp": peer},
                device_id_type=pl.DeviceIdType.MESH,
            ).start()
            return carry

        lax.fori_loop(1, groups, start, 0)
        target[me] = source[me]

        def finish(i, carry):
            peer = lax.rem(me + i, groups)
            origin = lax.rem(me + groups - i, groups)
            pltpu.make_async_remote_copy(
                src_ref=source.at[peer],
                dst_ref=target.at[origin],
                send_sem=send_sems.at[i],
                recv_sem=recv_sems.at[i],
                device_id={"tp": peer},
                device_id_type=pl.DeviceIdType.MESH,
            ).wait()
            return carry

        lax.fori_loop(1, groups, finish, 0)

    exchange(sent_ref, got_ref, send0, recv0)
    attend_kernel(allowed, keep, got_ref, cache_ref, att_ref, pairs_ref)
    exchange(att_ref, back_ref, send1, recv1)


def attend_slots(owners, lengths, accepts, ids, outgoing, cached):
    groups, slot_rows, lanes = outgoing.shape
    slots, cached_len, width = cached.shape
    vmem = pl.BlockSpec(memory_space=pltpu.VMEM)
    return pl.pallas_call(
        exchange_kernel,
        out_shape=(
            jax.ShapeDtypeStruct((groups, slot_rows, HD), jnp.bfloat16),
            jax.ShapeDtypeStruct((slot_rows, width), jnp.bfloat16),
            jax.ShapeDtypeStruct((1, slot_rows), jnp.int32),
        ),
        in_specs=[vmem] * 6,
        out_specs=(vmem, vmem, vmem),
        scratch_shapes=[
            pltpu.VMEM((groups, slot_rows, lanes), jnp.bfloat16),
            pltpu.VMEM((groups, slot_rows, HD), jnp.bfloat16),
            pltpu.SemaphoreType.DMA((groups,)),
            pltpu.SemaphoreType.DMA((groups,)),
            pltpu.SemaphoreType.DMA((groups,)),
            pltpu.SemaphoreType.DMA((groups,)),
        ],
        compiler_params=pltpu.CompilerParams(collective_id=2, has_side_effects=True),
    )(owners, lengths, accepts, ids, outgoing, cached.reshape(slots * cached_len, width))


def reduce_kernel(
    owner_ref, heads_ref, hid_ref, wo_hbm, out_ref,
    p_ref, wo_ref, res_ref, got0, got1, stage0, stage1,
    load_sem, shift_send, shift_recv, send_sems, recv_sems,
):
    me = lax.axis_index("tp")
    section = lax.axis_index("section")
    sections = lax.axis_size("section")
    after = lax.rem(section + 1, sections)
    before = lax.rem(section + sections - 1, sections)
    mx = me // NY
    my = lax.rem(me, NY)
    near = neighbours(mx, my)
    width = hid_ref.shape[1]
    parts = splits(width)
    got = (got0, got1)
    stage = (stage0, stage1)
    load = pltpu.make_async_copy(wo_hbm, wo_ref, load_sem)
    load.start()
    barrier = pltpu.get_barrier_semaphore()
    for device in near.values():
        pl.semaphore_signal(
            barrier, inc=1, device_id={"tp": device}, device_id_type=pl.DeviceIdType.MESH
        )
    pl.semaphore_signal(
        barrier, inc=1, device_id={"section": before}, device_id_type=pl.DeviceIdType.MESH
    )
    groups, count = p_ref.shape[:2]
    tokens = groups * count
    slot_rows = heads_ref.shape[0] * heads_ref.shape[1]
    chosen = slot_matrix(owner_ref, tokens, slot_rows)
    heads = lax.dot_general(
        chosen, heads_ref[...].reshape(slot_rows, heads_ref.shape[2]),
        (((0,), (0,)), ((), ())), preferred_element_type=jnp.float32,
    ).astype(jnp.bfloat16)
    load.wait()
    step = 256

    def multiply(mode):
        start, size = parts[mode]

        def one(k, carry):
            cols = pl.ds(pl.multiple_of(start + k * step, LANES), step)
            piece = jnp.dot(heads, wo_ref[:, cols], preferred_element_type=jnp.float32)
            p_ref[:, :, cols] = piece.reshape(groups, count, step).astype(jnp.bfloat16)
            return carry

        lax.fori_loop(0, size // step, one, 0, unroll=True)

    started = []

    def total(mode, dx, dy):
        start, size = parts[mode]
        block = block_at(mx, my, dx, dy)
        summed = p_ref[block, :, pl.ds(start, size)].astype(jnp.float32)
        for link in children(mode, dx, dy):
            slot = place_of(*moved(*link, dx, dy))
            pltpu.make_async_remote_copy(
                src_ref=stage[mode].at[slot],
                dst_ref=got[mode].at[slot],
                send_sem=send_sems.at[mode, slot],
                recv_sem=recv_sems.at[mode, slot],
                device_id={"tp": near[link]},
                device_id_type=pl.DeviceIdType.MESH,
            ).wait_recv()
            summed = summed + got[mode][slot].astype(jnp.float32)
        return summed

    def send(mode, dx, dy, source):
        slot = place_of(dx, dy)
        axis, sign = parent(mode, dx, dy)
        sent = pltpu.make_async_remote_copy(
            src_ref=source,
            dst_ref=got[mode].at[slot],
            send_sem=send_sems.at[mode, slot],
            recv_sem=recv_sems.at[mode, slot],
            device_id={"tp": near[axis, -sign]},
            device_id_type=pl.DeviceIdType.MESH,
        )
        sent.start()
        started.append(sent)

    def send_leaf(mode, dx, dy):
        start, size = parts[mode]
        send(mode, dx, dy, p_ref.at[block_at(mx, my, dx, dy), :, pl.ds(start, size)])

    def shift(mode):
        start, size = parts[mode]
        cols = pl.ds(start, size)
        return pltpu.make_async_remote_copy(
            src_ref=res_ref.at[:, cols],
            dst_ref=out_ref.at[:, cols],
            send_sem=shift_send.at[mode],
            recv_sem=shift_recv.at[mode],
            device_id={"section": after},
            device_id_type=pl.DeviceIdType.MESH,
        )

    order = arrival_order([part[1] * 16 / 46e3 for part in parts])[::-1]
    multiply(1)
    pl.semaphore_wait(barrier, len(near) + 1)
    early = [event for event in order[:16] if event[0] == 1 and not children(*event)]
    for event in early:
        send_leaf(*event)
    multiply(0)
    for event in order:
        if event in early:
            continue
        mode, dx, dy = event
        start, size = parts[mode]
        if (dx, dy) == (0, 0):
            cols = pl.ds(start, size)
            summed = total(mode, dx, dy) + hid_ref[:, cols].astype(jnp.float32)
            res_ref[:, cols] = summed.astype(jnp.bfloat16)
            shift(mode).start()
        elif children(mode, dx, dy):
            slot = place_of(dx, dy)
            stage[mode][slot] = total(mode, dx, dy).astype(jnp.bfloat16)
            send(mode, dx, dy, stage[mode].at[slot])
        else:
            send_leaf(mode, dx, dy)
    for sent in started:
        sent.wait_send()
    for mode in (0, 1):
        shift(mode).wait()


def reduce_rows(owners, heads, residual, weight_out):
    count, width = residual.shape
    groups = NX * NY
    parts = splits(width)
    vmem = pl.BlockSpec(memory_space=pltpu.VMEM)
    return pl.pallas_call(
        reduce_kernel,
        out_shape=jax.ShapeDtypeStruct((count, width), jnp.bfloat16),
        in_specs=[vmem, vmem, vmem, pl.BlockSpec(memory_space=pl.ANY)],
        out_specs=vmem,
        scratch_shapes=[
            pltpu.VMEM((groups, count, width), jnp.bfloat16),
            pltpu.VMEM(weight_out.shape, jnp.bfloat16),
            pltpu.VMEM((count, width), jnp.bfloat16),
            pltpu.VMEM((groups, count, parts[0][1]), jnp.bfloat16),
            pltpu.VMEM((groups, count, parts[1][1]), jnp.bfloat16),
            pltpu.VMEM((groups, count, parts[0][1]), jnp.bfloat16),
            pltpu.VMEM((groups, count, parts[1][1]), jnp.bfloat16),
            pltpu.SemaphoreType.DMA,
            pltpu.SemaphoreType.DMA((2,)),
            pltpu.SemaphoreType.DMA((2,)),
            pltpu.SemaphoreType.DMA((2, groups)),
            pltpu.SemaphoreType.DMA((2, groups)),
        ],
        compiler_params=pltpu.CompilerParams(collective_id=1, has_side_effects=True),
    )(owners, heads, residual, weight_out)


def on_device(
    hidden, norm_gain, w_query, w_keyval, w_out, kv_cache, owner_map, accepted, context, draft_ids
):
    slot_rows = kv_cache.shape[1] * draft_ids.shape[2]
    outgoing = project_rows(
        hidden[0], norm_gain, owner_map, w_query[0], w_keyval[0], slot_rows
    )
    returned, committed, kept_ids = attend_slots(
        owner_map, context, accepted, draft_ids[0].T, outgoing, kv_cache[0]
    )
    shifted = reduce_rows(owner_map, returned, hidden[0], w_out[0])
    return (shifted[None], committed[None], kept_ids)


def solution(mesh):
    placed = (
        P("section", "tp", None),
        P("section", None),
        P("section", None, "tp"),
        P("section", "tp", None),
        P("section", "tp", None),
        P("section", "tp", None, None),
        P("section", None),
        P("section", None),
        P("section", None),
        P("section", None, None),
    )
    return jax.shard_map(
        on_device,
        mesh=mesh,
        in_specs=placed,
        out_specs=(P("section", "tp", None), P("section", "tp", None), P("section", "tp")),
        check_vma=False,
    )
```

```python
import jax
import jax.numpy as jnp
from jax import lax
from jax.experimental import pallas as pl
from jax.experimental.pallas import tpu as pltpu
from jax.sharding import PartitionSpec as P

HEADS = 32
KVH = 4
HD = 128


epsilon = 1e-06


NX = 4
NY = 8
LANES = 128
XY_SHARE = 26 / 64


def splits(width):
    first = max(1, round(width // LANES * XY_SHARE)) * LANES
    return ((0, first), (first, width - first))


def far_positive(mode, axis, dx, dy):
    if mode == 0:
        return True if axis == 0 else dx % 2 == 0
    return dy % 2 == 0 if axis == 0 else False


def reach(mode, axis, sign, dx, dy):
    half = (NX if axis == 0 else NY) // 2
    return half if far_positive(mode, axis, dx, dy) == (sign > 0) else half - 1


def travelled(mode, axis, dx, dy):
    size = NX if axis == 0 else NY
    ahead = (-dx if axis == 0 else -dy) % size
    if ahead == 0:
        return 0
    if ahead <= reach(mode, axis, 1, dx, dy):
        return ahead
    return ahead - size


def children(mode, dx, dy):
    first, second = (0, 1) if mode == 0 else (1, 0)
    hops = []
    step1 = travelled(mode, first, dx, dy)
    step2 = travelled(mode, second, dx, dy)
    if step2 == 0:
        for sign in (1, -1):
            if step1 * sign >= 0 and abs(step1) < reach(mode, first, sign, dx, dy):
                hops.append((first, sign))
    for sign in (1, -1):
        if step2 * sign >= 0 and abs(step2) < reach(mode, second, sign, dx, dy):
            hops.append((second, sign))
    return hops


def moved(axis, sign, dx, dy):
    return ((dx - sign) % NX, dy) if axis == 0 else (dx, (dy - sign) % NY)


def parent(mode, dx, dy):
    first, second = (0, 1) if mode == 0 else (1, 0)
    step2 = travelled(mode, second, dx, dy)
    axis = second if step2 else first
    return (axis, 1 if travelled(mode, axis, dx, dy) > 0 else -1)


def arrival_order(weights):
    free = {}
    order = []
    pending = [(0.0, 0, 0, 0), (0.0, 1, 0, 0)]
    while pending:
        pending.sort()
        now, mode, dx, dy = pending.pop(0)
        order.append((mode, dx, dy))
        for axis, sign in children(mode, dx, dy):
            begin = max(now, free.get((axis, sign), 0.0))
            free[axis, sign] = begin + weights[mode]
            pending.append((begin + weights[mode] + 1.6, mode) + moved(axis, sign, dx, dy))
    return order


def place_of(dx, dy):
    return dx * NY + dy


def neighbours(mx, my):
    return {
        (0, 1): lax.rem(mx + 1, NX) * NY + my,
        (0, -1): lax.rem(mx + NX - 1, NX) * NY + my,
        (1, 1): mx * NY + lax.rem(my + 1, NY),
        (1, -1): mx * NY + lax.rem(my + NY - 1, NY),
    }


def greet(devices):
    barrier = pltpu.get_barrier_semaphore()
    for device in devices:
        pl.semaphore_signal(
            barrier, inc=1, device_id={"tp": device}, device_id_type=pl.DeviceIdType.MESH
        )
    pl.semaphore_wait(barrier, len(devices))


def block_at(mx, my, dx, dy):
    return lax.rem(mx + dx, NX) * NY + lax.rem(my + dy, NY)


def as_column(row):
    size = row.shape[1]
    first = lax.broadcasted_iota(jnp.int32, (size, size), 0)
    second = lax.broadcasted_iota(jnp.int32, (size, size), 1)
    return jnp.sum(jnp.where(first == second, row, 0), axis=1, keepdims=True)


def slot_column(owners, capacity):
    size = owners.shape[1]
    column = as_column(owners)
    request = lax.broadcasted_iota(jnp.int32, (size, size), 0)
    other = lax.broadcasted_iota(jnp.int32, (size, size), 1)
    earlier = (column == owners) & (other < request)
    return column * capacity + jnp.sum(jnp.where(earlier, 1, 0), axis=1, keepdims=True)


def as_row(column):
    size = column.shape[0]
    first = lax.broadcasted_iota(jnp.int32, (size, size), 0)
    second = lax.broadcasted_iota(jnp.int32, (size, size), 1)
    return jnp.sum(jnp.where(first == second, column, 0), axis=0, keepdims=True)


def slot_matrix(owner_ref, tokens, rows):
    owners = owner_ref[...]
    requests = owners.shape[1]
    steps = tokens // requests
    capacity = rows // (NX * NY * steps)
    column = slot_column(owners, capacity)
    request = lax.broadcasted_iota(jnp.int32, (requests, tokens), 0)
    token = lax.broadcasted_iota(jnp.int32, (requests, tokens), 1)
    slots = jnp.sum(jnp.where(request == token // steps, column, 0), axis=0, keepdims=True)
    step = lax.broadcasted_iota(jnp.int32, (1, tokens), 1) % steps
    row = lax.broadcasted_iota(jnp.int32, (rows, tokens), 0)
    return jnp.where(row == slots * steps + step, 1.0, 0.0).astype(jnp.bfloat16)


def project_kernel(
    hid_ref, gain_ref, owner_ref, wq_hbm, wp_hbm, out_ref,
    x_ref, all_ref, wq_ref, wp_ref, turned_ref, acc_ref, chosen_ref, load_sems, send_sems, recv_sems,
):
    me = lax.axis_index("tp")
    mx = me // NY
    my = lax.rem(me, NY)
    near = neighbours(mx, my)
    width = hid_ref.shape[1]
    parts = splits(width)
    loads = [
        pltpu.make_async_copy(wq_hbm, wq_ref, load_sems.at[0]),
        pltpu.make_async_copy(wp_hbm, wp_ref, load_sems.at[1]),
    ]
    for load in loads:
        load.start()
    rows = hid_ref[...].astype(jnp.float32)
    inverse_rms = lax.rsqrt(jnp.mean(rows * rows, axis=1, keepdims=True) + epsilon)
    x_ref[...] = (rows * inverse_rms * gain_ref[...]).astype(jnp.bfloat16)
    greet(list(near.values()))

    def copy(mode, dx, dy, link):
        start, size = parts[mode]
        there = place_of(*moved(*link, dx, dy))
        cols = pl.ds(start, size)
        block = block_at(mx, my, dx, dy)
        source = x_ref.at[:, cols] if (dx, dy) == (0, 0) else all_ref.at[block, :, cols]
        return pltpu.make_async_remote_copy(
            src_ref=source,
            dst_ref=all_ref.at[block, :, cols],
            send_sem=send_sems.at[mode, there],
            recv_sem=recv_sems.at[mode, there],
            device_id={"tp": near[link]},
            device_id_type=pl.DeviceIdType.MESH,
        )

    started = []
    order = arrival_order([part[1] * 16 / 46e3 for part in parts])
    for mode, dx, dy in order:
        if (dx, dy) != (0, 0):
            start, size = parts[mode]
            landed = all_ref.at[block_at(mx, my, dx, dy), :, pl.ds(start, size)]
            pltpu.make_async_remote_copy(
                src_ref=landed,
                dst_ref=landed,
                send_sem=send_sems.at[mode, place_of(dx, dy)],
                recv_sem=recv_sems.at[mode, place_of(dx, dy)],
                device_id={"tp": near[parent(mode, dx, dy)]},
                device_id_type=pl.DeviceIdType.MESH,
            ).wait_recv()
        for link in children(mode, dx, dy):
            sent = copy(mode, dx, dy, link)
            sent.start()
            started.append(sent)
        if len(started) == 8:
            all_ref[me] = x_ref[...]
            chosen_ref[...] = slot_matrix(owner_ref, chosen_ref.shape[1], chosen_ref.shape[0])
            for load in loads:
                load.wait()
            turned_ref[...] = jnp.zeros_like(turned_ref)
            for k in range(8):
                cols = pl.ds(k * (width // 8), width // 8)
                turned_ref[cols, : wp_ref.shape[0]] = wp_ref[:, cols].T
    groups, count = all_ref.shape[:2]
    tokens = groups * count
    query_cols = wq_ref.shape[1]
    pair_cols = wp_ref.shape[0]
    step = width // 8
    acc_ref[...] = jnp.zeros_like(acc_ref)

    def add(k, carry):
        cols = pl.ds(pl.multiple_of(k * step, step), step)
        x = all_ref[:, :, cols].reshape(tokens, step)
        weights = jnp.concatenate([wq_ref[cols, :], turned_ref[cols, :]], axis=1)
        acc_ref[...] += jnp.dot(x, weights, preferred_element_type=jnp.float32)
        return carry

    lax.fori_loop(0, 8, add, 0, unroll=True)
    queries = acc_ref[:, :query_cols].astype(jnp.bfloat16)
    pairs = acc_ref[:, query_cols : query_cols + pair_cols].astype(jnp.bfloat16)
    lane = lax.broadcasted_iota(jnp.int32, (pair_cols, LANES), 1)
    source = lax.broadcasted_iota(jnp.int32, (pair_cols, LANES), 0)
    offset = lax.rem(me, LANES // pair_cols) * pair_cols
    spread = jnp.where(lane == source + offset, 1.0, 0.0).astype(jnp.bfloat16)
    placed = jnp.dot(pairs, spread, preferred_element_type=jnp.float32).astype(jnp.bfloat16)
    chosen = chosen_ref[...]
    out_shape = out_ref.shape[:2] + (LANES,)
    out_ref[:, :, :LANES] = (
        jnp.dot(chosen, queries, preferred_element_type=jnp.float32)
        .reshape(out_shape).astype(jnp.bfloat16)
    )
    out_ref[:, :, LANES:] = (
        jnp.dot(chosen, placed, preferred_element_type=jnp.float32)
        .reshape(out_shape).astype(jnp.bfloat16)
    )
    for sent in started:
        sent.wait_send()


def project_rows(hidden, gain, owners, weight_query, weight_pair, slot_rows):
    count, width = hidden.shape
    groups = NX * NY
    vmem = pl.BlockSpec(memory_space=pltpu.VMEM)
    hbm = pl.BlockSpec(memory_space=pl.ANY)
    query_cols = weight_query.shape[1]
    return pl.pallas_call(
        project_kernel,
        out_shape=jax.ShapeDtypeStruct((groups, slot_rows, 2 * LANES), jnp.bfloat16),
        in_specs=[vmem, vmem, vmem, hbm, hbm],
        out_specs=vmem,
        scratch_shapes=[
            pltpu.VMEM((count, width), jnp.bfloat16),
            pltpu.VMEM((groups, count, width), jnp.bfloat16),
            pltpu.VMEM(weight_query.shape, jnp.bfloat16),
            pltpu.VMEM(weight_pair.shape, jnp.bfloat16),
            pltpu.VMEM((width, LANES), jnp.bfloat16),
            pltpu.VMEM((groups * count, query_cols + LANES), jnp.float32),
            pltpu.VMEM((groups * slot_rows, groups * count), jnp.bfloat16),
            pltpu.SemaphoreType.DMA((2,)),
            pltpu.SemaphoreType.DMA((2, groups)),
            pltpu.SemaphoreType.DMA((2, groups)),
        ],
        compiler_params=pltpu.CompilerParams(collective_id=0, has_side_effects=True),
    )(hidden, gain, owners, weight_query, weight_pair)


def attend_kernel(allowed, keep, got_ref, cache_ref, out_ref, pairs_ref):
    slot_rows = got_ref.shape[1]
    per_kv = HEADS // KVH
    rows = per_kv * slot_rows
    pieces = got_ref.shape[0] // (2 * KVH)
    for e in range(KVH):
        cols = slice(e * HD, (e + 1) * HD)
        value_cols = slice((KVH + e) * HD, (KVH + e + 1) * HD)

        def joined(first):
            total = got_ref[first, :, LANES:].astype(jnp.float32)
            for i in range(1, pieces):
                total = total + got_ref[first + i, :, LANES:].astype(jnp.float32)
            return total.astype(jnp.bfloat16)

        new_keys = joined(e * pieces)
        new_values = joined((KVH + e) * pieces)
        pairs_ref[:, cols] = jnp.where(keep, new_keys, jnp.zeros_like(new_keys))
        pairs_ref[:, value_cols] = jnp.where(keep, new_values, jnp.zeros_like(new_values))
        keys = jnp.concatenate([cache_ref[:, cols], new_keys], axis=0)
        values = jnp.concatenate([cache_ref[:, value_cols], new_values], axis=0)
        queries = got_ref[e * per_kv : (e + 1) * per_kv, :, :LANES].reshape(rows, HD)
        scores = lax.dot_general(
            queries, keys, (((1,), (1,)), ((), ())), preferred_element_type=jnp.float32
        ) * HD ** (-0.5)
        scores = jnp.where(allowed, scores, -jnp.inf)
        weights = jnp.exp(scores - jnp.max(scores, axis=1, keepdims=True))
        probs = (weights / jnp.sum(weights, axis=1, keepdims=True)).astype(jnp.bfloat16)
        attended = jnp.dot(probs, values, preferred_element_type=jnp.float32)
        out_ref[e * per_kv : (e + 1) * per_kv] = attended.reshape(
            per_kv, slot_rows, HD
        ).astype(jnp.bfloat16)


def exchange_kernel(
    owner_ref, length_ref, accept_ref, id_ref, sent_ref, cache_ref,
    back_ref, pairs_ref, kept_ref, got_ref, att_ref, send0, recv0, send1, recv1,
):
    me = lax.axis_index("tp")
    groups = sent_ref.shape[0]
    barrier = pltpu.get_barrier_semaphore()

    def greet_one(i, carry):
        pl.semaphore_signal(
            barrier, inc=1, device_id={"tp": lax.rem(me + i, groups)},
            device_id_type=pl.DeviceIdType.MESH,
        )
        return carry

    lax.fori_loop(1, groups, greet_one, 0)
    slot_rows = sent_ref.shape[1]
    requests = owner_ref.shape[1]
    steps = id_ref.shape[0]
    slots = slot_rows // steps
    cached_rows = cache_ref.shape[0]
    cached_len = cached_rows // slots
    slot_row = as_row(slot_column(owner_ref[...], slots))
    row = lax.broadcasted_iota(jnp.int32, (slot_rows, requests), 0)
    mine = me * slots + row // steps == slot_row
    ids = jnp.zeros((slot_rows, requests), jnp.int32)
    for j in range(steps):
        ids = jnp.where(row % steps == j, id_ref[j : j + 1, :], ids)

    def held(values):
        return jnp.sum(jnp.where(mine, values, 0), axis=1, keepdims=True)

    lengths = held(length_ref[...])
    step = lax.broadcasted_iota(jnp.int32, (slot_rows, 1), 0) % steps
    keep = step < held(accept_ref[...])
    kept_ref[...] = as_row(jnp.where(keep, held(ids), -1))
    span = cached_rows + slot_rows
    row = lax.broadcasted_iota(jnp.int32, (slot_rows, span), 0)
    col = lax.broadcasted_iota(jnp.int32, (slot_rows, span), 1)
    fresh = col - cached_rows
    in_cache = (fresh < 0) & (col // cached_len == row // steps) & (col % cached_len < lengths)
    in_draft = (fresh >= 0) & (fresh // steps == row // steps) & (fresh <= row)
    flags = jnp.where(in_cache | in_draft, 1, 0)
    allowed = jnp.concatenate([flags] * (HEADS // KVH), axis=0) == 1
    pl.semaphore_wait(barrier, groups - 1)

    def exchange(source, target, send_sems, recv_sems):
        def start(i, carry):
            peer = lax.rem(me + i, groups)
            pltpu.make_async_remote_copy(
                src_ref=source.at[peer],
                dst_ref=target.at[me],
                send_sem=send_sems.at[i],
                recv_sem=recv_sems.at[i],
                device_id={"tp": peer},
                device_id_type=pl.DeviceIdType.MESH,
            ).start()
            return carry

        lax.fori_loop(1, groups, start, 0)
        target[me] = source[me]

        def finish(i, carry):
            peer = lax.rem(me + i, groups)
            origin = lax.rem(me + groups - i, groups)
            pltpu.make_async_remote_copy(
                src_ref=source.at[peer],
                dst_ref=target.at[origin],
                send_sem=send_sems.at[i],
                recv_sem=recv_sems.at[i],
                device_id={"tp": peer},
                device_id_type=pl.DeviceIdType.MESH,
            ).wait()
            return carry

        lax.fori_loop(1, groups, finish, 0)

    exchange(sent_ref, got_ref, send0, recv0)
    attend_kernel(allowed, keep, got_ref, cache_ref, att_ref, pairs_ref)
    exchange(att_ref, back_ref, send1, recv1)


def attend_slots(owners, lengths, accepts, ids, outgoing, cached):
    groups, slot_rows, lanes = outgoing.shape
    slots, cached_len, width = cached.shape
    vmem = pl.BlockSpec(memory_space=pltpu.VMEM)
    return pl.pallas_call(
        exchange_kernel,
        out_shape=(
            jax.ShapeDtypeStruct((groups, slot_rows, HD), jnp.bfloat16),
            jax.ShapeDtypeStruct((slot_rows, width), jnp.bfloat16),
            jax.ShapeDtypeStruct((1, slot_rows), jnp.int32),
        ),
        in_specs=[vmem] * 6,
        out_specs=(vmem, vmem, vmem),
        scratch_shapes=[
            pltpu.VMEM((groups, slot_rows, lanes), jnp.bfloat16),
            pltpu.VMEM((groups, slot_rows, HD), jnp.bfloat16),
            pltpu.SemaphoreType.DMA((groups,)),
            pltpu.SemaphoreType.DMA((groups,)),
            pltpu.SemaphoreType.DMA((groups,)),
            pltpu.SemaphoreType.DMA((groups,)),
        ],
        compiler_params=pltpu.CompilerParams(collective_id=2, has_side_effects=True),
    )(owners, lengths, accepts, ids, outgoing, cached.reshape(slots * cached_len, width))


def reduce_kernel(
    owner_ref, heads_ref, hid_ref, wo_hbm, out_ref,
    p_ref, wo_ref, res_ref, got0, got1, stage0, stage1,
    load_sem, shift_send, shift_recv, send_sems, recv_sems,
):
    me = lax.axis_index("tp")
    section = lax.axis_index("section")
    sections = lax.axis_size("section")
    after = lax.rem(section + 1, sections)
    before = lax.rem(section + sections - 1, sections)
    mx = me // NY
    my = lax.rem(me, NY)
    near = neighbours(mx, my)
    width = hid_ref.shape[1]
    parts = splits(width)
    got = (got0, got1)
    stage = (stage0, stage1)
    load = pltpu.make_async_copy(wo_hbm, wo_ref, load_sem)
    load.start()
    barrier = pltpu.get_barrier_semaphore()
    for device in near.values():
        pl.semaphore_signal(
            barrier, inc=1, device_id={"tp": device}, device_id_type=pl.DeviceIdType.MESH
        )
    pl.semaphore_signal(
        barrier, inc=1, device_id={"section": before}, device_id_type=pl.DeviceIdType.MESH
    )
    groups, count = p_ref.shape[:2]
    tokens = groups * count
    slot_rows = heads_ref.shape[0] * heads_ref.shape[1]
    chosen = slot_matrix(owner_ref, tokens, slot_rows)
    heads = lax.dot_general(
        chosen, heads_ref[...].reshape(slot_rows, heads_ref.shape[2]),
        (((0,), (0,)), ((), ())), preferred_element_type=jnp.float32,
    ).astype(jnp.bfloat16)
    load.wait()
    step = 256

    def multiply(mode):
        start, size = parts[mode]

        def one(k, carry):
            cols = pl.ds(pl.multiple_of(start + k * step, LANES), step)
            piece = jnp.dot(heads, wo_ref[:, cols], preferred_element_type=jnp.float32)
            p_ref[:, :, cols] = piece.reshape(groups, count, step).astype(jnp.bfloat16)
            return carry

        lax.fori_loop(0, size // step, one, 0, unroll=True)

    started = []

    def total(mode, dx, dy):
        start, size = parts[mode]
        block = block_at(mx, my, dx, dy)
        summed = p_ref[block, :, pl.ds(start, size)].astype(jnp.float32)
        for link in children(mode, dx, dy):
            slot = place_of(*moved(*link, dx, dy))
            pltpu.make_async_remote_copy(
                src_ref=stage[mode].at[slot],
                dst_ref=got[mode].at[slot],
                send_sem=send_sems.at[mode, slot],
                recv_sem=recv_sems.at[mode, slot],
                device_id={"tp": near[link]},
                device_id_type=pl.DeviceIdType.MESH,
            ).wait_recv()
            summed = summed + got[mode][slot].astype(jnp.float32)
        return summed

    def send(mode, dx, dy, source):
        slot = place_of(dx, dy)
        axis, sign = parent(mode, dx, dy)
        sent = pltpu.make_async_remote_copy(
            src_ref=source,
            dst_ref=got[mode].at[slot],
            send_sem=send_sems.at[mode, slot],
            recv_sem=recv_sems.at[mode, slot],
            device_id={"tp": near[axis, -sign]},
            device_id_type=pl.DeviceIdType.MESH,
        )
        sent.start()
        started.append(sent)

    def send_leaf(mode, dx, dy):
        start, size = parts[mode]
        send(mode, dx, dy, p_ref.at[block_at(mx, my, dx, dy), :, pl.ds(start, size)])

    def shift(mode):
        start, size = parts[mode]
        cols = pl.ds(start, size)
        return pltpu.make_async_remote_copy(
            src_ref=res_ref.at[:, cols],
            dst_ref=out_ref.at[:, cols],
            send_sem=shift_send.at[mode],
            recv_sem=shift_recv.at[mode],
            device_id={"section": after},
            device_id_type=pl.DeviceIdType.MESH,
        )

    order = arrival_order([part[1] * 16 / 46e3 for part in parts])[::-1]
    multiply(1)
    pl.semaphore_wait(barrier, len(near) + 1)
    early = [event for event in order[:16] if event[0] == 1 and not children(*event)]
    for event in early:
        send_leaf(*event)
    multiply(0)
    for event in order:
        if event in early:
            continue
        mode, dx, dy = event
        start, size = parts[mode]
        if (dx, dy) == (0, 0):
            cols = pl.ds(start, size)
            summed = total(mode, dx, dy) + hid_ref[:, cols].astype(jnp.float32)
            res_ref[:, cols] = summed.astype(jnp.bfloat16)
            shift(mode).start()
        elif children(mode, dx, dy):
            slot = place_of(dx, dy)
            stage[mode][slot] = total(mode, dx, dy).astype(jnp.bfloat16)
            send(mode, dx, dy, stage[mode].at[slot])
        else:
            send_leaf(mode, dx, dy)
    for sent in started:
        sent.wait_send()
    for mode in (0, 1):
        shift(mode).wait()


def reduce_rows(owners, heads, residual, weight_out):
    count, width = residual.shape
    groups = NX * NY
    parts = splits(width)
    vmem = pl.BlockSpec(memory_space=pltpu.VMEM)
    return pl.pallas_call(
        reduce_kernel,
        out_shape=jax.ShapeDtypeStruct((count, width), jnp.bfloat16),
        in_specs=[vmem, vmem, vmem, pl.BlockSpec(memory_space=pl.ANY)],
        out_specs=vmem,
        scratch_shapes=[
            pltpu.VMEM((groups, count, width), jnp.bfloat16),
            pltpu.VMEM(weight_out.shape, jnp.bfloat16),
            pltpu.VMEM((count, width), jnp.bfloat16),
            pltpu.VMEM((groups, count, parts[0][1]), jnp.bfloat16),
            pltpu.VMEM((groups, count, parts[1][1]), jnp.bfloat16),
            pltpu.VMEM((groups, count, parts[0][1]), jnp.bfloat16),
            pltpu.VMEM((groups, count, parts[1][1]), jnp.bfloat16),
            pltpu.SemaphoreType.DMA,
            pltpu.SemaphoreType.DMA((2,)),
            pltpu.SemaphoreType.DMA((2,)),
            pltpu.SemaphoreType.DMA((2, groups)),
            pltpu.SemaphoreType.DMA((2, groups)),
        ],
        compiler_params=pltpu.CompilerParams(collective_id=1, has_side_effects=True),
    )(owners, heads, residual, weight_out)


def on_device(
    hidden, norm_gain, w_query, w_keyval, w_out, kv_cache, owner_map, accepted, context, draft_ids
):
    slot_rows = kv_cache.shape[1] * draft_ids.shape[2]
    outgoing = project_rows(
        hidden[0], norm_gain, owner_map, w_query[0], w_keyval[0], slot_rows
    )
    returned, committed, kept_ids = attend_slots(
        owner_map, context, accepted, draft_ids[0].T, outgoing, kv_cache[0]
    )
    shifted = reduce_rows(owner_map, returned, hidden[0], w_out[0])
    return (shifted[None], committed[None], kept_ids)


def solution(mesh):
    placed = (
        P("section", "tp", None),
        P("section", None),
        P("section", None, "tp"),
        P("section", "tp", None),
        P("section", "tp", None),
        P("section", "tp", None, None),
        P("section", None),
        P("section", None),
        P("section", None),
        P("section", None, None),
    )
    return jax.shard_map(
        on_device,
        mesh=mesh,
        in_specs=placed,
        out_specs=(P("section", "tp", None), P("section", "tp", None), P("section", "tp")),
        check_vma=False,
    )
```
